256 devices in a mesh: leaf: 8 (over x, core), turn: 32 (over z, y).
Axes of the slice: x: 4, y: 4, z: 8, core: 2. Of those that a mesh axis runs over, the one named last changes fastest.
Arguments:
- echoes: bfloat16 [16384, 256, 256], P(('leaf', 'turn')), may hold values from -6 to 6
- chirp: bfloat16 [2, 128], replicated, may hold values from -0.375 to 0.375
- taps: int32 [3, 2, 128, 8], replicated, may hold values from 0 to 127, as said below
- slots: int32 [8, 32], P('leaf'), may hold values from 0 to 31, each once within a row
Outputs:
- image: bfloat16 [128, 256, 256], P('leaf', 'turn')
The draws below stay inside these ranges and needn't reach their ends.
Inputs may be any that keep to these rules, and one draw needn't show every extreme that they name: Each row of taps is 8 consecutive beam indices starting at a - 4 + s with s from -3 to 3, clipped to the beams. Each row of slots is a permutation.
All inputs are finite; a program needn't handle non-finite values.
Results may differ from the reference program's by a relative error of at most 0.008.
Values may be sent and summed in bfloat16 or wider, within the bound.
A program may use at most 128 MiB of HBM per device.

```python
import math
from functools import partial
import jax
import jax.numpy as jnp
from jax import lax

CHIRP = 128
SUBP = 64
BEAMS = 128
TAPS = 8
PG = 2048
NSUB = 32
PULSES = 16384
NBLK = 256
LEVELS = 3
N_LEAF = 8


def draw_taps(key, part):
    shifts = jax.random.randint(key, (LEVELS, 2, BEAMS), -3, 4).astype(jnp.int32)
    base = jnp.arange(BEAMS, dtype=jnp.int32)[:, None] + jnp.arange(TAPS, dtype=jnp.int32)[None, :] - TAPS // 2
    return jnp.clip(base[None, None] + shifts[..., None], 0, BEAMS - 1).astype(jnp.int32)


def levels(rng, shape, pieces, low, top_value):
    def one(position, parts):
        draws = jax.random.uniform(jax.random.fold_in(jax.random.fold_in(rng, 6), position), (parts,), jnp.float32, low / len(pieces), top_value / len(pieces))
        return jnp.repeat(jnp.exp(draws), shape[position] // parts).reshape((-1,) + (1,) * (len(shape) - position - 1))

    loudness = one(*pieces[0])
    for cut in pieces[1:]:
        loudness = loudness * one(*cut)
    return loudness


def scatter_about(stream_key, extent, spread, limit, cuts=(), held_as=jnp.bfloat16):
    result = spread * jax.random.normal(stream_key, extent, jnp.float32)
    if cuts:
        result = result * levels(stream_key, extent, cuts, -0.22, 0.18)
    return jnp.clip(result, -limit, limit).astype(held_as)


def setup_inputs(seed: int = 0) -> dict:
    keys = jax.random.split(jax.random.key(seed), 5)
    return {
        "echoes": scatter_about(keys[0], (PULSES, NBLK, 2 * CHIRP), 1.0, 6.0, ((0, 256),)),
        "chirp": scatter_about(keys[1], (2, CHIRP), (2 * CHIRP) ** -0.5, 0.375),
        "taps": draw_taps(jax.random.fold_in(keys[4], 71), 0),
        "slots": jax.vmap(lambda own: jax.random.permutation(own, NSUB))(jax.random.split(keys[3], N_LEAF)).reshape((N_LEAF, NSUB)).astype(jnp.int32),
    }


WEIGHTS = (-1.0 / 32, 3.0 / 32, -7.0 / 32, 21.0 / 32, 21.0 / 32, -7.0 / 32, 3.0 / 32, -1.0 / 32)

def chirp_matrices(chirp):
    width = chirp.shape[1]
    rows = jnp.arange(width, dtype=jnp.int32)[:, None]
    cols = jnp.arange(width, dtype=jnp.int32)[None, :]
    offset = jnp.remainder(rows - cols, width)
    picks = (offset[:, :, None] == jnp.arange(width, dtype=jnp.int32)[None, None, :]).astype(jnp.float32)
    table = jnp.einsum('jik,ck->cji', picks, chirp.astype(jnp.float32), precision=lax.Precision.HIGHEST)
    lower = rows >= cols

    def complex_block(mask):
        real_part = jnp.where(mask, table[0], 0.0)
        imag_part = jnp.where(mask, table[1], 0.0)
        upper_half = jnp.concatenate([real_part, imag_part], axis=1)
        lower_half = jnp.concatenate([-imag_part, real_part], axis=1)
        return jnp.concatenate([upper_half, lower_half], axis=0).astype(jnp.bfloat16)
    return (complex_block(lower), complex_block(jnp.logical_not(lower)))

def compress(blocks, following, first_matrix, second_matrix):
    width = blocks.shape[-1]
    total = jnp.dot(blocks.reshape(-1, width), first_matrix, preferred_element_type=jnp.float32)
    total = total + jnp.dot(following.reshape(-1, width), second_matrix, preferred_element_type=jnp.float32)
    return total.astype(jnp.bfloat16).reshape(blocks.shape)

def steering(slot_row, beams, sub_len):
    count = slot_row.shape[0]
    beam = jnp.arange(beams, dtype=jnp.int32)[:, None, None]
    place = jnp.arange(sub_len, dtype=jnp.int32)[None, None, :]
    slot = slot_row.astype(jnp.int32)[None, :, None]
    period = 8 * sub_len
    phase_int = jnp.remainder((2 * beam + 1 - beams) * (2 * place + 1 - sub_len) + 3 * (beam + 1) * (2 * slot + 1) * (2 * place + 1), period)
    angle = phase_int.astype(jnp.float32) * (2.0 * math.pi / period)
    scale = 1.0 / math.sqrt(2.0 * count * sub_len)
    cos_part = (jnp.cos(angle) * scale).reshape(beams, count * sub_len)
    sin_part = (jnp.sin(angle) * scale).reshape(beams, count * sub_len)
    first = jnp.stack([cos_part, -sin_part], axis=1)
    second = jnp.stack([sin_part, cos_part], axis=1)
    return jnp.stack([first, second], axis=1).astype(jnp.bfloat16)

def backproject(data, steer):
    pulses, blocks, width = data.shape
    split = data.reshape(pulses, blocks, 2, width // 2)
    out = jnp.einsum('aecp,pbcj->abej', steer.astype(jnp.float32), split.astype(jnp.float32))
    return out.astype(jnp.bfloat16).reshape(steer.shape[0], blocks, width)

def merge_step(level_taps, level, side, first_block, child):
    beams, blocks, width = child.shape
    half = width // 2
    weights = jnp.array(WEIGHTS, jnp.float32)
    cells = jnp.arange(beams, dtype=jnp.int32)
    beam = cells[:, None, None]
    bins = (first_block * half + jnp.arange(blocks * half, dtype=jnp.int32)).reshape(1, blocks, half)
    picks = (level_taps[side][:, :, None] == cells[None, None, :]).astype(jnp.float32)
    matrix = jnp.einsum('atk,t->ak', picks, weights, precision=lax.Precision.HIGHEST)
    moved = jnp.dot(matrix, child.astype(jnp.float32).reshape(beams, -1), precision=lax.Precision.HIGHEST).reshape(beams, blocks, 2, half)
    sign = 2 * side - 1
    phase_int = jnp.remainder((2 * beam + 1 - beams) * (bins + 1) * (sign * (level + 2)) + beam * beam * (side + 1), 4096)
    angle = phase_int.astype(jnp.float32) * (2.0 * math.pi / 4096)
    cos_part = jnp.cos(angle)
    sin_part = jnp.sin(angle)
    real_part = cos_part * moved[:, :, 0] - sin_part * moved[:, :, 1]
    imag_part = cos_part * moved[:, :, 1] + sin_part * moved[:, :, 0]
    return jnp.stack([real_part, imag_part], axis=2).reshape(beams, blocks, width)

def merge_pair(level_taps, level, first_block, left, right):
    return merge_step(level_taps, level, 0, first_block, left) + merge_step(level_taps, level, 1, first_block, right)

def reference(echoes, chirp, taps, slots):
    first_matrix, second_matrix = chirp_matrices(chirp)
    width = echoes.shape[2]
    groups = echoes.reshape(N_LEAF, PG, NBLK, width)

    def one_group(pair):
        block, slot_row = pair
        following = jnp.concatenate([block[:, 1:], jnp.zeros((PG, 1, width), jnp.bfloat16)], axis=1)
        compressed = compress(block, following, first_matrix, second_matrix)
        return backproject(compressed, steering(slot_row, BEAMS, SUBP))
    images = lax.map(one_group, (groups, slots)).astype(jnp.float32)
    for level in range(LEVELS):
        step_fn = jax.vmap(partial(merge_pair, taps[level], level, 0))
        images = step_fn(images[0::2], images[1::2])
    return images[0].astype(jnp.bfloat16)
```

```python
import functools
import math

import jax
import jax.numpy as jnp
from jax import lax
from jax.experimental import pallas as pl
from jax.experimental.pallas import tpu as pltpu
from jax.sharding import PartitionSpec as P

WEIGHTS = (-1.0 / 32, 3.0 / 32, -7.0 / 32, 21.0 / 32, 21.0 / 32, -7.0 / 32, 3.0 / 32, -1.0 / 32)
MESH = pl.DeviceIdType.MESH

BEAMS = 128
TAPS = 8
SUBP = 64
NSUB = 32
NZ = 8
NY = 4
NLEAF = 8
TILES = NZ * NY
COLS = 512
WIDE = 2 * COLS
BY = 80
BZ = BEAMS - BY
GRAN = 16
NGRAN = 256 // GRAN

f32 = jnp.float32
bf16 = jnp.bfloat16


def cos_sin(n):
    n = n & 4095
    quad = (n + 512) >> 10
    m = (n - (quad << 10)).astype(f32) * (2.0 * math.pi / 4096)
    m2 = m * m
    s = m * (1.0 + m2 * (-1.0 / 6 + m2 * (1.0 / 120 + m2 * (-1.0 / 5040 + m2 * (1.0 / 362880)))))
    c = 1.0 + m2 * (-0.5 + m2 * (1.0 / 24 + m2 * (-1.0 / 720 + m2 * (1.0 / 40320))))
    odd = (quad & 1) == 1
    cc = jnp.where(odd, s, c)
    ss = jnp.where(odd, c, s)
    cos = jnp.where((quad == 1) | (quad == 2), -cc, cc)
    sin = jnp.where((quad == 2) | (quad == 3), -ss, ss)
    return cos, sin


def iota(shape, dim):
    return lax.broadcasted_iota(jnp.int32, shape, dim)


def prep_kernel(chirp_ref, taps_ref, slots_ref, mc_ref, a_ref, d0_ref, i12_ref, d12_ref):
    leaf = lax.axis_index("leaf")
    turn = lax.axis_index("turn")
    core = leaf % 2
    sq = (BEAMS, BEAMS)

    g = jnp.broadcast_to(chirp_ref[...][:, None, :], (2, 8, 128)).reshape(16, 128)
    flip = ((iota(sq, 0) + iota(sq, 1)) % 128 == 0).astype(bf16)
    h = jnp.dot(g, flip, preferred_element_type=f32)
    lower = iota(sq, 0) >= iota(sq, 1)
    tabs = []
    for part in range(2):
        row = jnp.broadcast_to(h[8 * part : 8 * part + 1], sq)
        tabs.append(pltpu.roll(row, 0, 1, stride=1, stride_axis=0))
    for side in range(2):
        re, im = (jnp.where(lower if side == 0 else ~lower, t, 0.0) for t in tabs)
        at = 256 * side
        mc_ref[0:128, at : at + 128] = re.astype(bf16)
        mc_ref[0:128, at + 128 : at + 256] = im.astype(bf16)
        mc_ref[128:256, at : at + 128] = (-im).astype(bf16)
        mc_ref[128:256, at + 128 : at + 256] = re.astype(bf16)

    def interp(level, side):
        rows = taps_ref[level, side]
        cells = iota(sq, 1)
        total = jnp.zeros(sq, f32)
        for t in range(TAPS):
            total = total + jnp.where(rows[:, t : t + 1] == cells, WEIGHTS[t], 0.0)
        return total.astype(bf16)

    slot = slots_ref[0, turn]
    beam = iota(sq, 0)
    lane = iota(sq, 1)
    m = lane % SUBP
    n = (2 * beam + 1 - BEAMS) * (2 * m + 1 - SUBP) + 3 * (beam + 1) * (2 * slot + 1) * (2 * m + 1)
    cos, sin = cos_sin(8 * n)
    scale = 1.0 / math.sqrt(2.0 * NSUB * SUBP)
    cos, sin = cos * scale, sin * scale
    first = lane < SUBP
    s_re = jnp.where(first, cos, -sin).astype(bf16)
    s_im = jnp.where(first, sin, cos).astype(bf16)
    i0 = interp(0, core)
    z_re = jnp.dot(i0, s_re, preferred_element_type=f32)
    z_im = jnp.dot(i0, s_im, preferred_element_type=f32)
    ca, sa = cos_sin(beam * beam * (core + 1))
    a_ref[0:128] = (ca * z_re - sa * z_im).astype(bf16)
    a_ref[128:256] = (ca * z_im + sa * z_re).astype(bf16)

    big = (BEAMS, COLS)
    bins = iota(big, 1) + COLS * core + 1
    odd = 2 * iota(big, 0) + 1 - BEAMS
    sign = (2 * core - 1).astype(f32)
    for par in range(2):
        c, s = cos_sin(2 * odd * (bins + 1024 * par))
        d0_ref[0, par] = c
        d0_ref[1, par] = s * sign

    bins = bins + 1024 * turn
    for level in (1, 2):
        side = (leaf >> level) % 2
        i12_ref[level - 1] = interp(level, side)
        square = iota(big, 0) * iota(big, 0)
        c, s = cos_sin(odd * bins * ((2 * side - 1) * (level + 2)) + square * (side + 1))
        d12_ref[level - 1, 0] = c
        d12_ref[level - 1, 1] = s


def prepare(chirp, taps, slots):
    vmem = pl.BlockSpec(memory_space=pltpu.VMEM)
    return pl.pallas_call(
        prep_kernel,
        out_shape=(
            jax.ShapeDtypeStruct((256, 512), bf16),
            jax.ShapeDtypeStruct((256, 128), bf16),
            jax.ShapeDtypeStruct((2, 2, BEAMS, COLS), f32),
            jax.ShapeDtypeStruct((2, BEAMS, BEAMS), bf16),
            jax.ShapeDtypeStruct((2, 2, BEAMS, COLS), f32),
        ),
        in_specs=[vmem, vmem, pl.BlockSpec(memory_space=pltpu.SMEM)],
        out_specs=(vmem,) * 5,
        name="prepare",
    )(chirp, taps, slots)


def main_kernel(
    x_ref, mc_ref, a_ref, d0_ref, i12_ref, d12_ref, out_ref,
    xbuf, u, edge, xb, aoth, ay, az,
    rby, sby, rbz, sbz, rb2, sb2, rb3, sb3, img, vout, rl,
    in_sem, ex_s, ex_r, a_s, a_r, y_s, y_r, z_s, z_r, s2_s, s2_r, s3_s, s3_r, l_s, l_r,
):
    leaf = lax.axis_index("leaf")
    turn = lax.axis_index("turn")
    core = leaf % 2
    z = turn // NY
    y = turn % NY
    mate = leaf + 1 - 2 * core

    def turn_at(zz, yy):
        return (zz % NZ) * NY + yy % NY

    ynbr = (turn_at(z, y + 1), turn_at(z, y + NY - 1))
    znbr = (turn_at(z + 1, y), turn_at(z + NZ - 1, y))

    def pull(gi, slot):
        at = pl.multiple_of(gi * GRAN, GRAN)
        return pltpu.make_async_copy(x_ref.at[:, pl.ds(at, GRAN), :], xbuf.at[slot], in_sem.at[slot])

    pull(NGRAN - 1, 0).start()

    barrier = pltpu.get_barrier_semaphore()
    for t in ynbr + znbr:
        pl.semaphore_signal(barrier, inc=1, device_id={"turn": t}, device_id_type=MESH)
    for e in range(1, NLEAF):
        pl.semaphore_signal(barrier, inc=1, device_id={"leaf": (leaf + e) % NLEAF}, device_id_type=MESH)
    pl.semaphore_wait(barrier, 4 + NLEAF - 1)

    def remote(src, dst, ssem, rsem, where):
        return pltpu.make_async_remote_copy(
            src_ref=src, dst_ref=dst, send_sem=ssem, recv_sem=rsem,
            device_id=where, device_id_type=MESH,
        )

    a_copy = remote(a_ref, aoth, a_s, a_r, {"leaf": mate})
    a_copy.start()

    def exchange(gi):
        pair = pl.ds(2 * gi, 2)
        return remote(xb.at[pair, 2], xb.at[pair, 1], ex_s.at[gi], ex_r.at[gi], {"leaf": mate})

    edge[...] = jnp.zeros_like(edge)

    def granule(step, carry):
        gi = NGRAN - 1 - step
        slot = step % 2

        @pl.when(step + 1 < NGRAN)
        def _():
            pull(gi - 1, 1 - slot).start()

        pull(gi, slot).wait()
        for hf in range(2):
            rows = xbuf[slot, pl.ds(32 * hf, 32)].reshape(32 * GRAN, 256)
            prod = jnp.dot(rows, mc_ref[...], preferred_element_type=f32)
            for q in range(4):
                u[q, 512 * hf : 512 * hf + 512, :] = prod[:, 128 * q : 128 * q + 128]
        for b in range(GRAN):
            half = b % 8 // 4
            plane = 2 * (core if half == 0 else 1 - core)
            tile = 2 * gi + b // 8
            at = 128 * (b % 4)
            for q in range(2):
                own = u[q, pl.ds(b, SUBP, stride=GRAN), :]
                if b == GRAN - 1:
                    nxt = edge[q]
                else:
                    nxt = u[2 + q, pl.ds(b + 1, SUBP, stride=GRAN), :]
                xb[tile, plane, 64 * q : 64 * q + 64, at : at + 128] = (own + nxt).astype(bf16)
        for q in range(2):
            edge[q] = u[2 + q, pl.ds(0, SUBP, stride=GRAN), :]
        exchange(gi).start()
        return carry

    lax.fori_loop(0, NGRAN, granule, 0)

    a_copy.wait()
    for ref, low, count in ((ay, 0, BY), (az, BY, BZ)):
        for part in range(2):
            rows = slice(128 * part + low, 128 * part + low + count)
            mine, other = a_ref[rows], aoth[rows]
            ref[part * count : (part + 1) * count, 0:128] = mine
            ref[part * count : (part + 1) * count, 128:256] = other
            ref[(2 + part) * count : (3 + part) * count, 0:128] = mine
            ref[(2 + part) * count : (3 + part) * count, 128:256] = -other

    rby[:, 12] = jnp.zeros((2, BY, WIDE), bf16)
    rbz[:, 14] = jnp.zeros((2, BZ, WIDE), bf16)
    for d in range(2):
        unsent = slice(COLS, WIDE) if d == 0 else slice(0, COLS)
        rb2[d, 0, :, unsent] = jnp.zeros((BY, COLS), bf16)
        rb3[d, 0, :, unsent] = jnp.zeros((BZ, COLS), bf16)

    def drain(gi, carry):
        exchange(gi).wait()
        return carry

    lax.fori_loop(0, NGRAN, drain, 0)

    def partial_image(ref, low, count, tile, adds, put):
        par = tile % 2
        beams = slice(low, low + count)
        for at in range(0, COLS, 256):
            cols = slice(at, at + 256)
            imag = slice(COLS + at, COLS + at + 256)
            data = xb[tile, 0:2, :, cols].reshape(256, 256)
            r = jnp.dot(ref[...], data, preferred_element_type=f32)
            c, s = d0_ref[0, par, beams, cols], d0_ref[1, par, beams, cols]
            re = c * r[0:count] - s * r[3 * count :]
            im = c * r[count : 2 * count] + s * r[2 * count : 3 * count]
            for got in adds:
                re = re + got[:, cols].astype(f32)
                im = im + got[:, imag].astype(f32)
            put(cols, re)
            put(imag, im)

    def put_to(ref):
        def put(cols, value):
            ref[:, cols] = value.astype(ref.dtype)
        return put

    def order(i, n):
        step = (i + 1) // 2
        return n // 2 + (1 - 2 * (i % 2)) * step

    def y_copy(d, k):
        return remote(sby.at[d, k], rby.at[d, k], y_s.at[d, k], y_r.at[d, k], {"turn": ynbr[d]})

    def z_copy(d, k):
        return remote(sbz.at[d, k], rbz.at[d, k], z_s.at[d, k], z_r.at[d, k], {"turn": znbr[d]})

    def y_message(d, k):
        far = k < 4
        away = jnp.where(far, 2, 1)
        i = jnp.where(far, k + 4 * d, k - 4)
        yy = y + away if d == 0 else y + NY - away
        tile = turn_at(z + order(i, NZ), yy)
        base = 4 + 4 * d
        takes = (k >= base) & (k < base + 4)
        src = jnp.where(takes, k - base, 12)

        @pl.when(takes)
        def _():
            y_copy(d, k - base).wait_recv()

        partial_image(ay, 0, BY, tile, (rby.at[d, src],), put_to(sby.at[d, k]))
        y_copy(d, k).start()

    def z_message(d, k):
        away = 4 - (k + 2) // 4
        i = (k + 2) % 4
        if d == 0:
            i = jnp.where(k < 2, k, i)
        zz = z + away if d == 0 else z + NZ - away
        tile = turn_at(zz, y + order(i, NY))
        if d == 0:
            takes = ((k >= 2) & (k < 4)) | (k >= 6)
            prev = jnp.where(k < 4, k - 2, k - 4)
        else:
            takes = k >= 4
            prev = k - 4
        src = jnp.where(takes, prev, 14)

        @pl.when(takes)
        def _():
            z_copy(d, prev).wait_recv()

        partial_image(az, BY, BZ, tile, (rbz.at[d, src],), put_to(sbz.at[d, k]))
        z_copy(d, k).start()

    def slot_loop(k, carry):
        @pl.when(k < 12)
        def _():
            for d in range(2):
                y_message(d, k)

        for d in range(2):
            z_message(d, k)
        return carry

    lax.fori_loop(0, 14, slot_loop, 0)

    halves = (slice(0, COLS), slice(COLS, WIDE))

    def far2(d):
        part = halves[d]
        return remote(sb2.at[d, 0, :, part], rb2.at[d, 0, :, part], s2_s.at[d, 0], s2_r.at[d, 0], {"turn": znbr[d]})

    def near2(d, k):
        return remote(sb2.at[d, k], rb2.at[d, k], s2_s.at[d, k], s2_r.at[d, k], {"turn": znbr[d]})

    def far3(d):
        part = halves[d]
        return remote(sb3.at[d, 0, :, part], rb3.at[d, 0, :, part], s3_s.at[d, 0], s3_r.at[d, 0], {"turn": ynbr[d]})

    def near3(d, k):
        return remote(sb3.at[d, k], rb3.at[d, k], s3_s.at[d, k], s3_r.at[d, k], {"turn": ynbr[d]})

    def wait_y(i):
        for d in range(2):
            y_copy(d, 4 + i).wait_recv()
        return (rby.at[0, 4 + i], rby.at[1, 4 + i])

    def wait_z(i):
        for d in range(2):
            z_copy(d, 10 + i).wait_recv()
        return (rbz.at[0, 10 + i], rbz.at[1, 10 + i])

    def put_both(ref):
        def put(cols, value):
            d = 0 if cols.start < COLS else 1
            ref[d, 0, :, cols] = value.astype(bf16)
        return put

    partial_image(ay, 0, BY, turn_at(z + 4, y), wait_y(0), put_both(sb2))
    for d in range(2):
        far2(d).start()

    def second_y(d, q):
        i = 2 * q + 1 + d
        adds = wait_y(i)

        @pl.when(q == 0)
        def _():
            far2(d).wait_recv()

        @pl.when(q > 0)
        def _():
            near2(d, q).wait_recv()

        partial_image(ay, 0, BY, turn_at(z + order(i, NZ), y), adds + (rb2.at[d, q],), put_to(sb2.at[d, q + 1]))
        near2(d, q + 1).start()

    def second_z(i):
        adds = wait_z(i)
        tile = turn_at(z, y + (2, 1, 3, 0)[i])
        if i == 0:
            partial_image(az, BY, BZ, tile, adds, put_both(sb3))
            for d in range(2):
                far3(d).start()
        elif i < 3:
            d = i - 1
            far3(d).wait_recv()
            partial_image(az, BY, BZ, tile, adds + (rb3.at[d, 0],), put_to(sb3.at[d, 1]))
            near3(d, 1).start()
        else:
            for d in range(2):
                near3(d, 1).wait_recv()
            adds = adds + (rb3.at[0, 1], rb3.at[1, 1])
            partial_image(az, BY, BZ, tile, adds, put_to(img.at[pl.ds(BY, BZ)]))

    def second_loop(q, carry):
        for d in range(2):
            second_y(d, q)
        return carry

    lax.fori_loop(0, 2, second_loop, 0)
    for i in range(3):
        second_z(i)
    lax.fori_loop(2, 3, second_loop, 0)
    second_z(3)
    adds = wait_y(7)
    for d in range(2):
        near2(d, 3).wait_recv()
    partial_image(ay, 0, BY, turn, adds + (rb2.at[0, 3], rb2.at[1, 3]), put_to(img.at[pl.ds(0, BY)]))

    for level in range(2):
        value = img[...]
        high = value.astype(bf16)
        low = (value - high.astype(f32)).astype(bf16)
        matrix = i12_ref[level]
        moved = jnp.dot(matrix, high, preferred_element_type=f32) + jnp.dot(matrix, low, preferred_element_type=f32)
        c, s = d12_ref[level, 0], d12_ref[level, 1]
        re = c * moved[:, :COLS] - s * moved[:, COLS:]
        im = c * moved[:, COLS:] + s * moved[:, :COLS]
        target = img if level == 0 else vout
        target[:, :COLS] = re.astype(target.dtype)
        target[:, COLS:] = im.astype(target.dtype)

    def share(e):
        to = (leaf + e) % NLEAF
        rows = pl.ds(pl.multiple_of(16 * to, 16), 16)
        return remote(vout.at[rows], rl.at[leaf], l_s.at[e - 1], l_r.at[e - 1], {"leaf": to})

    def shared(e):
        src = (leaf + NLEAF - e) % NLEAF
        return remote(vout.at[pl.ds(0, 16)], rl.at[src], l_s.at[e - 1], l_r.at[e - 1], {"leaf": mate})

    for e in range(1, NLEAF):
        share(e).start()
    rl[leaf] = vout[pl.ds(pl.multiple_of(16 * leaf, 16), 16)]
    for e in range(1, NLEAF):
        shared(e).wait_recv()
    for side in range(2):
        total = rl[side].astype(f32)
        for xx in range(1, 4):
            total = total + rl[2 * xx + side].astype(f32)
        total = total.astype(bf16)
        for b in range(4):
            out_ref[4 * side + b, :, 0:128] = total[:, 128 * b : 128 * b + 128]
            out_ref[4 * side + b, :, 128:256] = total[:, COLS + 128 * b : COLS + 128 * b + 128]

    def sent_y(k, carry):
        for d in range(2):
            y_copy(d, k).wait_send()
        return carry

    def sent_z(k, carry):
        for d in range(2):
            z_copy(d, k).wait_send()
        return carry

    lax.fori_loop(0, 12, sent_y, 0)
    lax.fori_loop(0, 14, sent_z, 0)
    for d in range(2):
        far2(d).wait_send()
        far3(d).wait_send()
        near3(d, 1).wait_send()
        for k in range(1, 4):
            near2(d, k).wait_send()
    for e in range(1, NLEAF):
        share(e).wait_send()


def reduce_merge(x, mc, a, d0, i12, d12):
    vmem = pl.BlockSpec(memory_space=pltpu.VMEM)
    dma = pltpu.SemaphoreType.DMA
    return pl.pallas_call(
        main_kernel,
        out_shape=jax.ShapeDtypeStruct((8, 16, 256), bf16),
        in_specs=[pl.BlockSpec(memory_space=pl.ANY)] + [vmem] * 5,
        out_specs=vmem,
        scratch_shapes=[
            pltpu.VMEM((2, SUBP, GRAN, 256), bf16),
            pltpu.VMEM((4, SUBP * GRAN, 128), f32),
            pltpu.VMEM((2, SUBP, 128), f32),
            pltpu.VMEM((TILES, 3, 128, COLS), bf16),
            pltpu.VMEM((256, 128), bf16),
            pltpu.VMEM((4 * BY, 256), bf16),
            pltpu.VMEM((4 * BZ, 256), bf16),
            pltpu.VMEM((2, 13, BY, WIDE), bf16),
            pltpu.VMEM((2, 12, BY, WIDE), bf16),
            pltpu.VMEM((2, 15, BZ, WIDE), bf16),
            pltpu.VMEM((2, 14, BZ, WIDE), bf16),
            pltpu.VMEM((2, 4, BY, WIDE), bf16),
            pltpu.VMEM((2, 4, BY, WIDE), bf16),
            pltpu.VMEM((2, 2, BZ, WIDE), bf16),
            pltpu.VMEM((2, 2, BZ, WIDE), bf16),
            pltpu.VMEM((BEAMS, WIDE), f32),
            pltpu.VMEM((BEAMS, WIDE), bf16),
            pltpu.VMEM((NLEAF, 16, WIDE), bf16),
            dma((2,)), dma((NGRAN,)), dma((NGRAN,)), dma, dma,
            dma((2, 12)), dma((2, 12)), dma((2, 14)), dma((2, 14)),
            dma((2, 4)), dma((2, 4)), dma((2, 2)), dma((2, 2)),
            dma((NLEAF - 1,)), dma((NLEAF - 1,)),
        ],
        compiler_params=pltpu.CompilerParams(
            collective_id=0, has_side_effects=True, vmem_limit_bytes=60 * 1024 * 1024
        ),
        name="reduce_merge",
    )(x, mc, a, d0, i12, d12)


def per_device(echoes, chirp, taps, slots):
    tables = prepare(chirp, taps, slots)
    image = reduce_merge(echoes, *tables)
    return jnp.transpose(image, (1, 0, 2))


def solution(mesh):
    placed = (P(("leaf", "turn"), None, None), P(), P(), P("leaf", None))
    return jax.shard_map(
        per_device, mesh=mesh, in_specs=placed, out_specs=P("leaf", "turn", None), check_vma=False
    )
```

```python
import functools
import math

import jax
import jax.numpy as jnp
from jax import lax
from jax.experimental import pallas as pl
from jax.experimental.pallas import tpu as pltpu
from jax.sharding import PartitionSpec as P

WEIGHTS = (-1.0 / 32, 3.0 / 32, -7.0 / 32, 21.0 / 32, 21.0 / 32, -7.0 / 32, 3.0 / 32, -1.0 / 32)
MESH = pl.DeviceIdType.MESH

BEAMS = 128
TAPS = 8
SUBP = 64
NSUB = 32
NZ = 8
NY = 4
NLEAF = 8
TILES = NZ * NY
COLS = 512
WIDE = 2 * COLS
BY = 80
BZ = BEAMS - BY
GRAN = 16
NGRAN = 256 // GRAN

f32 = jnp.float32
bf16 = jnp.bfloat16


def cos_sin(n):
    n = n & 4095
    quad = (n + 512) >> 10
    m = (n - (quad << 10)).astype(f32) * (2.0 * math.pi / 4096)
    m2 = m * m
    s = m * (1.0 + m2 * (-1.0 / 6 + m2 * (1.0 / 120 + m2 * (-1.0 / 5040 + m2 * (1.0 / 362880)))))
    c = 1.0 + m2 * (-0.5 + m2 * (1.0 / 24 + m2 * (-1.0 / 720 + m2 * (1.0 / 40320))))
    odd = (quad & 1) == 1
    cc = jnp.where(odd, s, c)
    ss = jnp.where(odd, c, s)
    cos = jnp.where((quad == 1) | (quad == 2), -cc, cc)
    sin = jnp.where((quad == 2) | (quad == 3), -ss, ss)
    return cos, sin


def iota(shape, dim):
    return lax.broadcasted_iota(jnp.int32, shape, dim)


def prep_kernel(chirp_ref, taps_ref, slots_ref, mc_ref, a_ref, d0_ref, i12_ref, d12_ref):
    leaf = lax.axis_index("leaf")
    turn = lax.axis_index("turn")
    core = leaf % 2
    sq = (BEAMS, BEAMS)

    g = jnp.broadcast_to(chirp_ref[...][:, None, :], (2, 8, 128)).reshape(16, 128)
    flip = ((iota(sq, 0) + iota(sq, 1)) % 128 == 0).astype(bf16)
    h = jnp.dot(g, flip, preferred_element_type=f32)
    lower = iota(sq, 0) >= iota(sq, 1)
    tabs = []
    for part in range(2):
        row = jnp.broadcast_to(h[8 * part : 8 * part + 1], sq)
        tabs.append(pltpu.roll(row, 0, 1, stride=1, stride_axis=0))
    for side in range(2):
        re, im = (jnp.where(lower if side == 0 else ~lower, t, 0.0) for t in tabs)
        at = 256 * side
        mc_ref[0:128, at : at + 128] = re.astype(bf16)
        mc_ref[0:128, at + 128 : at + 256] = im.astype(bf16)
        mc_ref[128:256, at : at + 128] = (-im).astype(bf16)
        mc_ref[128:256, at + 128 : at + 256] = re.astype(bf16)

    def interp(level, side):
        rows = taps_ref[level, side]
        cells = iota(sq, 1)
        total = jnp.zeros(sq, f32)
        for t in range(TAPS):
            total = total + jnp.where(rows[:, t : t + 1] == cells, WEIGHTS[t], 0.0)
        return total.astype(bf16)

    slot = slots_ref[0, turn]
    beam = iota(sq, 0)
    lane = iota(sq, 1)
    m = lane % SUBP
    n = (2 * beam + 1 - BEAMS) * (2 * m + 1 - SUBP) + 3 * (beam + 1) * (2 * slot + 1) * (2 * m + 1)
    cos, sin = cos_sin(8 * n)
    scale = 1.0 / math.sqrt(2.0 * NSUB * SUBP)
    cos, sin = cos * scale, sin * scale
    first = lane < SUBP
    s_re = jnp.where(first, cos, -sin).astype(bf16)
    s_im = jnp.where(first, sin, cos).astype(bf16)
    i0 = interp(0, core)
    z_re = jnp.dot(i0, s_re, preferred_element_type=f32)
    z_im = jnp.dot(i0, s_im, preferred_element_type=f32)
    ca, sa = cos_sin(beam * beam * (core + 1))
    a_ref[0:128] = (ca * z_re - sa * z_im).astype(bf16)
    a_ref[128:256] = (ca * z_im + sa * z_re).astype(bf16)

    big = (BEAMS, COLS)
    bins = iota(big, 1) + COLS * core + 1
    odd = 2 * iota(big, 0) + 1 - BEAMS
    sign = (2 * core - 1).astype(f32)
    for par in range(2):
        c, s = cos_sin(2 * odd * (bins + 1024 * par))
        d0_ref[0, par] = c
        d0_ref[1, par] = s * sign

    bins = bins + 1024 * turn
    for level in (1, 2):
        side = (leaf >> level) % 2
        i12_ref[level - 1] = interp(level, side)
        square = iota(big, 0) * iota(big, 0)
        c, s = cos_sin(odd * bins * ((2 * side - 1) * (level + 2)) + square * (side + 1))
        d12_ref[level - 1, 0] = c
        d12_ref[level - 1, 1] = s


def prepare(chirp, taps, slots):
    vmem = pl.BlockSpec(memory_space=pltpu.VMEM)
    return pl.pallas_call(
        prep_kernel,
        out_shape=(
            jax.ShapeDtypeStruct((256, 512), bf16),
            jax.ShapeDtypeStruct((256, 128), bf16),
            jax.ShapeDtypeStruct((2, 2, BEAMS, COLS), f32),
            jax.ShapeDtypeStruct((2, BEAMS, BEAMS), bf16),
            jax.ShapeDtypeStruct((2, 2, BEAMS, COLS), f32),
        ),
        in_specs=[vmem, vmem, pl.BlockSpec(memory_space=pltpu.SMEM)],
        out_specs=(vmem,) * 5,
        name="prepare",
    )(chirp, taps, slots)


def main_kernel(
    x_ref, mc_ref, a_ref, d0_ref, i12_ref, d12_ref, out_ref,
    xbuf, ebuf, u, edge, edges, xb, aoth, ay, az,
    rby, sby, rbz, sbz, rb2, sb2, rb3, sb3, img, vout, rl,
    in_sem, e_sem, ex_s, ex_r, a_s, a_r, y_s, y_r, z_s, z_r, s2_s, s2_r, s3_s, s3_r, l_s, l_r,
):
    leaf = lax.axis_index("leaf")
    turn = lax.axis_index("turn")
    core = leaf % 2
    z = turn // NY
    y = turn % NY
    mate = leaf + 1 - 2 * core

    def turn_at(zz, yy):
        return (zz % NZ) * NY + yy % NY

    ynbr = (turn_at(z, y + 1), turn_at(z, y + NY - 1))
    znbr = (turn_at(z + 1, y), turn_at(z + NZ - 1, y))

    def order(i, n):
        step = (i + 1) // 2
        return n // 2 + (1 - 2 * (i % 2)) * step

    def chunk(i):
        return (z + order(i, NZ)) % NZ

    def pull(i, g):
        at = pl.multiple_of((2 * chunk(i) + 1 - g) * GRAN, GRAN)
        return pltpu.make_async_copy(x_ref.at[:, pl.ds(at, GRAN), :], xbuf.at[i % 2, g], in_sem.at[i % 2, g])

    def pull_edge(i):
        at = pl.multiple_of((chunk(i) + 1) % NZ * 2 * GRAN, 8)
        slot = i // 2 % 2
        return pltpu.make_async_copy(x_ref.at[:, pl.ds(at, 8), :], ebuf.at[slot], e_sem.at[slot])

    pull_edge(0).start()
    for g in range(2):
        pull(0, g).start()

    barrier = pltpu.get_barrier_semaphore()
    for t in ynbr + znbr:
        pl.semaphore_signal(barrier, inc=1, device_id={"turn": t}, device_id_type=MESH)
    for e in range(1, NLEAF):
        pl.semaphore_signal(barrier, inc=1, device_id={"leaf": (leaf + e) % NLEAF}, device_id_type=MESH)
    pl.semaphore_wait(barrier, 4 + NLEAF - 1)

    def remote(src, dst, ssem, rsem, where):
        return pltpu.make_async_remote_copy(
            src_ref=src, dst_ref=dst, send_sem=ssem, recv_sem=rsem,
            device_id=where, device_id_type=MESH,
        )

    a_copy = remote(a_ref, aoth, a_s, a_r, {"leaf": mate})
    a_copy.start()

    def exchange(i):
        four = pl.ds(4 * chunk(i), 4)
        return remote(xb.at[four, 2], xb.at[four, 1], ex_s.at[i], ex_r.at[i], {"leaf": mate})

    def granule(i, g):
        pull(i, g).wait()
        gi = 2 * chunk(i) + 1 - g
        for hf in range(2):
            rows = xbuf[i % 2, g, pl.ds(32 * hf, 32)].reshape(32 * GRAN, 256)
            prod = jnp.dot(rows, mc_ref[...], preferred_element_type=f32).reshape(32, 2, 8, 512)
            for q in range(4):
                for e in range(2):
                    part = prod[:, e, :, 128 * q : 128 * q + 128].reshape(256, 128)
                    u[q, e, 256 * hf : 256 * hf + 256, :] = part
        for b in range(GRAN):
            half = b % 8 // 4
            plane = 2 * (core if half == 0 else 1 - core)
            tile = 2 * gi + b // 8
            at = 128 * (b % 4)
            for q in range(2):
                own = u[q, b // 8, pl.ds(b % 8, SUBP, stride=8), :]
                if b == GRAN - 1:
                    nxt = edge[q]
                else:
                    nxt = u[2 + q, (b + 1) // 8, pl.ds((b + 1) % 8, SUBP, stride=8), :]
                xb[tile, plane, 64 * q : 64 * q + 64, at : at + 128] = (own + nxt).astype(bf16)
        for q in range(2):
            edge[q] = u[2 + q, 0, pl.ds(0, SUBP, stride=8), :]

    def compress(i):
        @pl.when(i + 1 < NZ)
        def _():
            for g in range(2):
                pull(i + 1, g).start()

        @pl.when((i % 2 == 1) & (i + 1 < NZ))
        def _():
            pull_edge(i + 1).start()

        here = chunk(i)

        @pl.when(i % 2 == 0)
        def _():
            pull_edge(i).wait()
            rows = ebuf[i // 2 % 2].reshape(SUBP * 8, 256)
            prod = jnp.dot(rows, mc_ref[:, 256:512], preferred_element_type=f32)
            for q in range(2):
                u[q, 0] = prod[:, 128 * q : 128 * q + 128]
            for q in range(2):
                edges[(here + 1) % NZ, q] = u[q, 0, pl.ds(0, SUBP, stride=8), :]

        edge[...] = edges[here + 1]

        def both(g, carry):
            granule(i, g)
            return carry

        lax.fori_loop(0, 2, both, 0)
        edges[here] = edge[...]
        exchange(i).start()

    edges[NZ] = jnp.zeros((2, SUBP, 128), f32)
    compress(0)

    a_copy.wait()
    for ref, low, count in ((ay, 0, BY), (az, BY, BZ)):
        for part in range(2):
            rows = slice(128 * part + low, 128 * part + low + count)
            mine, other = a_ref[rows], aoth[rows]
            ref[part * count : (part + 1) * count, 0:128] = mine
            ref[part * count : (part + 1) * count, 128:256] = other
            ref[(2 + part) * count : (3 + part) * count, 0:128] = mine
            ref[(2 + part) * count : (3 + part) * count, 128:256] = -other

    rby[:, 12] = jnp.zeros((2, BY, WIDE), bf16)
    rbz[:, 14] = jnp.zeros((2, BZ, WIDE), bf16)
    for d in range(2):
        unsent = slice(COLS, WIDE) if d == 0 else slice(0, COLS)
        rb2[d, 0, :, unsent] = jnp.zeros((BY, COLS), bf16)
        rb3[d, 0, :, unsent] = jnp.zeros((BZ, COLS), bf16)

    def partial_image(ref, low, count, tile, adds, put):
        par = tile % 2
        beams = slice(low, low + count)
        for at in range(0, COLS, 256):
            cols = slice(at, at + 256)
            imag = slice(COLS + at, COLS + at + 256)
            data = xb[tile, 0:2, :, cols].reshape(256, 256)
            r = jnp.dot(ref[...], data, preferred_element_type=f32)
            c, s = d0_ref[0, par, beams, cols], d0_ref[1, par, beams, cols]
            re = c * r[0:count] - s * r[3 * count :]
            im = c * r[count : 2 * count] + s * r[2 * count : 3 * count]
            for got in adds:
                re = re + got[:, cols].astype(f32)
                im = im + got[:, imag].astype(f32)
            put(cols, re)
            put(imag, im)

    def put_to(ref):
        def put(cols, value):
            ref[:, cols] = value.astype(ref.dtype)
        return put

    def y_to(d):
        return turn_at(z, y + 1 + 2 * d)

    def z_to(d):
        return turn_at(z + 1 + (NZ - 2) * d, y)

    def y_copy(d, k):
        return remote(sby.at[d, k], rby.at[d, k], y_s.at[d, k], y_r.at[d, k], {"turn": y_to(d)})

    def z_copy(d, k):
        return remote(sbz.at[d, k], rbz.at[d, k], z_s.at[d, k], z_r.at[d, k], {"turn": z_to(d)})

    def y_message(c, near, d):
        k = jnp.where(near == 1, 4 + c, c // 2)
        takes = (near == 1) & (c % 2 == d)
        src = jnp.where(takes, c // 2, 12)

        @pl.when(takes)
        def _():
            y_copy(d, c // 2).wait_recv()

        tile = turn_at(chunk(c), y + 2 + near * (2 * d - 1))
        partial_image(ay, 0, BY, tile, (rby.at[d, src],), put_to(sby.at[d, k]))
        y_copy(d, k).start()

    def z_far(d, j):
        tile = turn_at(chunk(0), y + order(j + 2 * d, NY))
        partial_image(az, BY, BZ, tile, (), put_to(sbz.at[d, j]))
        z_copy(d, j).start()

    def z_near(c, j):
        d = (c + 1) % 2
        step = (c - 1) // 2
        k = 2 + 4 * step + j
        takes = (step > 0) | (j // 2 == d)
        prev = jnp.where(step > 0, k - 4, j - 2 * d)
        src = jnp.where(takes, prev, 14)

        @pl.when(takes)
        def _():
            z_copy(d, prev).wait_recv()

        tile = turn_at(chunk(c), y + order(j, NY))
        partial_image(az, BY, BZ, tile, (rbz.at[d, src],), put_to(sbz.at[d, k]))
        z_copy(d, k).start()

    halves = (slice(0, COLS), slice(COLS, WIDE))

    def far2(d):
        part = halves[d]
        return remote(sb2.at[d, 0, :, part], rb2.at[d, 0, :, part], s2_s.at[d, 0], s2_r.at[d, 0], {"turn": z_to(d)})

    def near2(d, k):
        return remote(sb2.at[d, k], rb2.at[d, k], s2_s.at[d, k], s2_r.at[d, k], {"turn": z_to(d)})

    def far3(d):
        part = halves[d]
        return remote(sb3.at[d, 0, :, part], rb3.at[d, 0, :, part], s3_s.at[d, 0], s3_r.at[d, 0], {"turn": y_to(d)})

    def near3(d, k):
        return remote(sb3.at[d, k], rb3.at[d, k], s3_s.at[d, k], s3_r.at[d, k], {"turn": y_to(d)})

    def wait_y(i):
        for d in range(2):
            y_copy(d, 4 + i).wait_recv()
        return (rby.at[0, 4 + i], rby.at[1, 4 + i])

    def wait_z(i):
        for d in range(2):
            z_copy(d, 10 + i).wait_recv()
        return (rbz.at[0, 10 + i], rbz.at[1, 10 + i])

    def put_both(ref):
        def put(cols, value):
            d = 0 if cols.start < COLS else 1
            ref[d, 0, :, cols] = value.astype(bf16)
        return put

    def second_far():
        partial_image(ay, 0, BY, turn_at(z + 4, y), wait_y(0), put_both(sb2))
        for d in range(2):
            far2(d).start()

    def second_y(i):
        d = (i + 1) % 2
        q = (i - 1) // 2
        adds = wait_y(i)
        for side in range(2):
            @pl.when((q == 0) & (d == side))
            def _():
                far2(side).wait_recv()

        @pl.when(q > 0)
        def _():
            near2(d, q).wait_recv()

        partial_image(ay, 0, BY, turn_at(chunk(i), y), adds + (rb2.at[d, q],), put_to(sb2.at[d, q + 1]))
        near2(d, q + 1).start()

    def second_z(i):
        adds = wait_z(i)
        tile = turn_at(z, y + (2, 1, 3, 0)[i])
        if i == 0:
            partial_image(az, BY, BZ, tile, adds, put_both(sb3))
            for d in range(2):
                far3(d).start()
        elif i < 3:
            d = i - 1
            far3(d).wait_recv()
            partial_image(az, BY, BZ, tile, adds + (rb3.at[d, 0],), put_to(sb3.at[d, 1]))
            near3(d, 1).start()
        else:
            for d in range(2):
                near3(d, 1).wait_recv()
            adds = adds + (rb3.at[0, 1], rb3.at[1, 1])
            partial_image(az, BY, BZ, tile, adds, put_to(img.at[pl.ds(BY, BZ)]))

    def main_loop(i, carry):
        @pl.when(i < NZ)
        def _():
            compress(i)

        @pl.when(i <= NZ)
        def _():
            c = i - 1
            exchange(c).wait_recv()

            def pair(near, carry):
                y_message(c, near, (c + near) % 2)
                return carry

            lax.fori_loop(0, 2, pair, 0)

        @pl.when(i == 1)
        def _():
            def far(n, carry):
                z_far(n // 2, n % 2)
                return carry

            lax.fori_loop(0, 4, far, 0)

        @pl.when((i >= 3) & (i <= NZ))
        def _():
            def near(j, carry):
                z_near(i - 2, j)
                return carry

            lax.fori_loop(0, 4, near, 0)

        @pl.when(i >= 4)
        def _():
            y_message(i - 4, 1, i % 2)

        @pl.when(i == NZ)
        def _():
            second_far()

        @pl.when(i > NZ)
        def _():
            second_y(i - NZ)

        return carry

    lax.fori_loop(1, 12, main_loop, 0)

    def second_loop(i, carry):
        second_y(i)
        return carry

    second_z(0)
    lax.fori_loop(4, 5, second_loop, 0)
    second_z(1)
    second_z(2)
    lax.fori_loop(5, 7, second_loop, 0)
    second_z(3)
    adds = wait_y(7)
    for d in range(2):
        near2(d, 3).wait_recv()
    partial_image(ay, 0, BY, turn, adds + (rb2.at[0, 3], rb2.at[1, 3]), put_to(img.at[pl.ds(0, BY)]))

    for level in range(2):
        value = img[...]
        high = value.astype(bf16)
        low = (value - high.astype(f32)).astype(bf16)
        matrix = i12_ref[level]
        moved = jnp.dot(matrix, high, preferred_element_type=f32) + jnp.dot(matrix, low, preferred_element_type=f32)
        c, s = d12_ref[level, 0], d12_ref[level, 1]
        re = c * moved[:, :COLS] - s * moved[:, COLS:]
        im = c * moved[:, COLS:] + s * moved[:, :COLS]
        target = img if level == 0 else vout
        target[:, :COLS] = re.astype(target.dtype)
        target[:, COLS:] = im.astype(target.dtype)

    def share(e):
        to = (leaf + e) % NLEAF
        rows = pl.ds(pl.multiple_of(16 * to, 16), 16)
        return remote(vout.at[rows], rl.at[leaf], l_s.at[e - 1], l_r.at[e - 1], {"leaf": to})

    def shared(e):
        src = (leaf + NLEAF - e) % NLEAF
        return remote(vout.at[pl.ds(0, 16)], rl.at[src], l_s.at[e - 1], l_r.at[e - 1], {"leaf": mate})

    for e in range(1, NLEAF):
        share(e).start()
    rl[leaf] = vout[pl.ds(pl.multiple_of(16 * leaf, 16), 16)]
    for e in range(1, NLEAF):
        shared(e).wait_recv()
    for side in range(2):
        total = rl[side].astype(f32)
        for xx in range(1, 4):
            total = total + rl[2 * xx + side].astype(f32)
        total = total.astype(bf16)
        for b in range(4):
            out_ref[4 * side + b, :, 0:128] = total[:, 128 * b : 128 * b + 128]
            out_ref[4 * side + b, :, 128:256] = total[:, COLS + 128 * b : COLS + 128 * b + 128]

    def sent_y(k, carry):
        for d in range(2):
            y_copy(d, k).wait_send()
        return carry

    def sent_z(k, carry):
        for d in range(2):
            z_copy(d, k).wait_send()
        return carry

    def sent_mate(i, carry):
        exchange(i).wait_send()
        return carry

    lax.fori_loop(0, NZ, sent_mate, 0)
    lax.fori_loop(0, 12, sent_y, 0)
    lax.fori_loop(0, 14, sent_z, 0)
    for d in range(2):
        far2(d).wait_send()
        far3(d).wait_send()
        near3(d, 1).wait_send()
        for k in range(1, 4):
            near2(d, k).wait_send()
    for e in range(1, NLEAF):
        share(e).wait_send()


def reduce_merge(x, mc, a, d0, i12, d12):
    vmem = pl.BlockSpec(memory_space=pltpu.VMEM)
    dma = pltpu.SemaphoreType.DMA
    return pl.pallas_call(
        main_kernel,
        out_shape=jax.ShapeDtypeStruct((8, 16, 256), bf16),
        in_specs=[pl.BlockSpec(memory_space=pl.ANY)] + [vmem] * 5,
        out_specs=vmem,
        scratch_shapes=[
            pltpu.VMEM((2, 2, SUBP, GRAN, 256), bf16),
            pltpu.VMEM((2, SUBP, 8, 256), bf16),
            pltpu.VMEM((4, 2, SUBP * 8, 128), f32),
            pltpu.VMEM((2, SUBP, 128), f32),
            pltpu.VMEM((NZ + 1, 2, SUBP, 128), f32),
            pltpu.VMEM((TILES, 3, 128, COLS), bf16),
            pltpu.VMEM((256, 128), bf16),
            pltpu.VMEM((4 * BY, 256), bf16),
            pltpu.VMEM((4 * BZ, 256), bf16),
            pltpu.VMEM((2, 13, BY, WIDE), bf16),
            pltpu.VMEM((2, 12, BY, WIDE), bf16),
            pltpu.VMEM((2, 15, BZ, WIDE), bf16),
            pltpu.VMEM((2, 14, BZ, WIDE), bf16),
            pltpu.VMEM((2, 4, BY, WIDE), bf16),
            pltpu.VMEM((2, 4, BY, WIDE), bf16),
            pltpu.VMEM((2, 2, BZ, WIDE), bf16),
            pltpu.VMEM((2, 2, BZ, WIDE), bf16),
            pltpu.VMEM((BEAMS, WIDE), f32),
            pltpu.VMEM((BEAMS, WIDE), bf16),
            pltpu.VMEM((NLEAF, 16, WIDE), bf16),
            dma((2, 2)), dma((2,)), dma((NZ,)), dma((NZ,)), dma, dma,
            dma((2, 12)), dma((2, 12)), dma((2, 14)), dma((2, 14)),
            dma((2, 4)), dma((2, 4)), dma((2, 2)), dma((2, 2)),
            dma((NLEAF - 1,)), dma((NLEAF - 1,)),
        ],
        compiler_params=pltpu.CompilerParams(
            collective_id=0, has_side_effects=True, vmem_limit_bytes=60 * 1024 * 1024
        ),
        name="reduce_merge",
    )(x, mc, a, d0, i12, d12)


def per_device(echoes, chirp, taps, slots):
    tables = prepare(chirp, taps, slots)
    image = reduce_merge(echoes, *tables)
    return jnp.transpose(image, (1, 0, 2))


def solution(mesh):
    placed = (P(("leaf", "turn"), None, None), P(), P(), P("leaf", None))
    return jax.shard_map(
        per_device, mesh=mesh, in_specs=placed, out_specs=P("leaf", "turn", None), check_vma=False
    )
```

```python
import functools
import math

import jax
import jax.numpy as jnp
from jax import lax
from jax.experimental import pallas as pl
from jax.experimental.pallas import tpu as pltpu
from jax.sharding import PartitionSpec as P

WEIGHTS = (-1.0 / 32, 3.0 / 32, -7.0 / 32, 21.0 / 32, 21.0 / 32, -7.0 / 32, 3.0 / 32, -1.0 / 32)
MESH = pl.DeviceIdType.MESH

BEAMS = 128
TAPS = 8
SUBP = 64
NSUB = 32
NZ = 8
NY = 4
NLEAF = 8
TILES = NZ * NY
COLS = 512
WIDE = 2 * COLS
BY = 80
BZ = BEAMS - BY
GRAN = 16
NGRAN = 256 // GRAN

f32 = jnp.float32
bf16 = jnp.bfloat16


def cos_sin(n):
    n = n & 4095
    quad = (n + 512) >> 10
    m = (n - (quad << 10)).astype(f32) * (2.0 * math.pi / 4096)
    m2 = m * m
    s = m * (1.0 + m2 * (-1.0 / 6 + m2 * (1.0 / 120 + m2 * (-1.0 / 5040 + m2 * (1.0 / 362880)))))
    c = 1.0 + m2 * (-0.5 + m2 * (1.0 / 24 + m2 * (-1.0 / 720 + m2 * (1.0 / 40320))))
    odd = (quad & 1) == 1
    cc = jnp.where(odd, s, c)
    ss = jnp.where(odd, c, s)
    cos = jnp.where((quad == 1) | (quad == 2), -cc, cc)
    sin = jnp.where((quad == 2) | (quad == 3), -ss, ss)
    return cos, sin


def iota(shape, dim):
    return lax.broadcasted_iota(jnp.int32, shape, dim)


def interp(rows):
    cells = iota((BEAMS, BEAMS), 0)
    total = jnp.zeros((BEAMS, BEAMS), f32)
    for t in range(TAPS):
        total = total + jnp.where(rows[t : t + 1, :] == cells, WEIGHTS[t], 0.0)
    return total.T.astype(bf16)


def phase_blocks(first, step, count):
    c, s = cos_sin(first)
    blocks = [(c, s)]
    fc, fs = cos_sin(step)
    for _ in range(count - 1):
        c, s = c * fc - s * fs, s * fc + c * fs
        blocks.append((c, s))
    return blocks


def prep_kernel(chirp_ref, taps_ref, slots_ref, mc_ref, a_ref, d0_ref):
    leaf = lax.axis_index("leaf")
    turn = lax.axis_index("turn")
    core = leaf % 2
    sq = (BEAMS, BEAMS)

    g = jnp.broadcast_to(chirp_ref[...][:, None, :], (2, 8, 128)).reshape(16, 128)
    flip = ((iota(sq, 0) + iota(sq, 1)) % 128 == 0).astype(bf16)
    h = jnp.dot(g, flip, preferred_element_type=f32)
    lower = iota(sq, 0) >= iota(sq, 1)
    tabs = []
    for part in range(2):
        row = jnp.broadcast_to(h[8 * part : 8 * part + 1], sq)
        tabs.append(pltpu.roll(row, 0, 1, stride=1, stride_axis=0))
    for side in range(2):
        re, im = (jnp.where(lower if side == 0 else ~lower, t, 0.0) for t in tabs)
        at = 256 * side
        mc_ref[0:128, at : at + 128] = re.astype(bf16)
        mc_ref[0:128, at + 128 : at + 256] = im.astype(bf16)
        mc_ref[128:256, at : at + 128] = (-im).astype(bf16)
        mc_ref[128:256, at + 128 : at + 256] = re.astype(bf16)

    slot = slots_ref[0, turn]
    beam = iota(sq, 0)
    lane = iota(sq, 1)
    m = lane % SUBP
    n = (2 * beam + 1 - BEAMS) * (2 * m + 1 - SUBP) + 3 * (beam + 1) * (2 * slot + 1) * (2 * m + 1)
    cos, sin = cos_sin(8 * n)
    scale = 1.0 / math.sqrt(2.0 * NSUB * SUBP)
    cos, sin = cos * scale, sin * scale
    first = lane < SUBP
    s_re = jnp.where(first, cos, -sin).astype(bf16)
    s_im = jnp.where(first, sin, cos).astype(bf16)
    i0 = interp(taps_ref[0, core])
    z_re = jnp.dot(i0, s_re, preferred_element_type=f32)
    z_im = jnp.dot(i0, s_im, preferred_element_type=f32)
    ca, sa = cos_sin(beam * beam * (core + 1))
    a_ref[0:128] = (ca * z_re - sa * z_im).astype(bf16)
    a_ref[128:256] = (ca * z_im + sa * z_re).astype(bf16)

    odd = 2 * beam + 1 - BEAMS
    sign = (2 * core - 1).astype(f32)
    blocks = phase_blocks(2 * odd * (lane + COLS * core + 1), 2 * odd * 128, COLS // 128)
    for b, (c, s) in enumerate(blocks):
        at = slice(128 * b, 128 * b + 128)
        d0_ref[0, 0, :, at] = c
        d0_ref[0, 1, :, at] = -c
        d0_ref[1, 0, :, at] = s * sign
        d0_ref[1, 1, :, at] = -s * sign


def prepare(chirp, taps, slots):
    vmem = pl.BlockSpec(memory_space=pltpu.VMEM)
    return pl.pallas_call(
        prep_kernel,
        out_shape=(
            jax.ShapeDtypeStruct((256, 512), bf16),
            jax.ShapeDtypeStruct((256, 128), bf16),
            jax.ShapeDtypeStruct((2, 2, BEAMS, COLS), f32),
        ),
        in_specs=[vmem, vmem, pl.BlockSpec(memory_space=pltpu.SMEM)],
        out_specs=(vmem,) * 3,
        name="prepare",
    )(chirp, taps, slots)


def main_kernel(
    x_ref, mc_ref, a_ref, d0_ref, taps_ref, out_ref,
    xbuf, ebuf, u, edge, edges, xb, aoth, ay, az,
    rby, sby, rbz, sbz, rb2, sb2, rb3, sb3, img, vout, rl, i12, d12,
    in_sem, e_sem, ex_s, ex_r, a_s, a_r, y_s, y_r, z_s, z_r, s2_s, s2_r, s3_s, s3_r, l_s, l_r,
):
    leaf = lax.axis_index("leaf")
    turn = lax.axis_index("turn")
    core = leaf % 2
    z = turn // NY
    y = turn % NY
    mate = leaf + 1 - 2 * core

    def turn_at(zz, yy):
        return (zz % NZ) * NY + yy % NY

    ynbr = (turn_at(z, y + 1), turn_at(z, y + NY - 1))
    znbr = (turn_at(z + 1, y), turn_at(z + NZ - 1, y))

    def order(i, n):
        step = (i + 1) // 2
        return n // 2 + (1 - 2 * (i % 2)) * step

    def chunk(i):
        return (z + order(i, NZ)) % NZ

    def pull(i, g):
        at = pl.multiple_of((2 * chunk(i) + 1 - g) * GRAN, GRAN)
        return pltpu.make_async_copy(x_ref.at[:, pl.ds(at, GRAN), :], xbuf.at[i % 2, g], in_sem.at[i % 2, g])

    def pull_edge(i):
        at = pl.multiple_of((chunk(i) + 1) % NZ * 2 * GRAN, 8)
        slot = i // 2 % 2
        return pltpu.make_async_copy(x_ref.at[:, pl.ds(at, 8), :], ebuf.at[slot], e_sem.at[slot])

    pull_edge(0).start()
    for g in range(2):
        pull(0, g).start()

    barrier = pltpu.get_barrier_semaphore()
    for t in ynbr + znbr:
        pl.semaphore_signal(barrier, inc=1, device_id={"turn": t}, device_id_type=MESH)
    for e in range(1, NLEAF):
        pl.semaphore_signal(barrier, inc=1, device_id={"leaf": (leaf + e) % NLEAF}, device_id_type=MESH)
    pl.semaphore_wait(barrier, 4 + NLEAF - 1)

    def remote(src, dst, ssem, rsem, where):
        return pltpu.make_async_remote_copy(
            src_ref=src, dst_ref=dst, send_sem=ssem, recv_sem=rsem,
            device_id=where, device_id_type=MESH,
        )

    a_copy = remote(a_ref, aoth, a_s, a_r, {"leaf": mate})
    a_copy.start()

    def exchange(i):
        four = pl.ds(4 * chunk(i), 4)
        return remote(xb.at[four, 2], xb.at[four, 1], ex_s.at[i], ex_r.at[i], {"leaf": mate})

    def granule(i, g):
        pull(i, g).wait()
        gi = 2 * chunk(i) + 1 - g
        for hf in range(2):
            rows = xbuf[i % 2, g, pl.ds(32 * hf, 32)].reshape(32 * GRAN, 256)
            prod = jnp.dot(rows, mc_ref[...], preferred_element_type=f32).reshape(32, 2, 8, 512)
            for q in range(4):
                for e in range(2):
                    part = prod[:, e, :, 128 * q : 128 * q + 128].reshape(256, 128)
                    u[q, e, 256 * hf : 256 * hf + 256, :] = part
        for b in range(GRAN):
            half = b % 8 // 4
            plane = 2 * (core if half == 0 else 1 - core)
            tile = 2 * gi + b // 8
            at = 128 * (b % 4)
            for q in range(2):
                own = u[q, b // 8, pl.ds(b % 8, SUBP, stride=8), :]
                if b == GRAN - 1:
                    nxt = edge[q]
                else:
                    nxt = u[2 + q, (b + 1) // 8, pl.ds((b + 1) % 8, SUBP, stride=8), :]
                xb[tile, plane, 64 * q : 64 * q + 64, at : at + 128] = (own + nxt).astype(bf16)
        for q in range(2):
            edge[q] = u[2 + q, 0, pl.ds(0, SUBP, stride=8), :]

    def compress(i):
        @pl.when(i + 1 < NZ)
        def _():
            for g in range(2):
                pull(i + 1, g).start()

        @pl.when((i % 2 == 1) & (i + 1 < NZ))
        def _():
            pull_edge(i + 1).start()

        here = chunk(i)

        @pl.when(i % 2 == 0)
        def _():
            pull_edge(i).wait()
            rows = ebuf[i // 2 % 2].reshape(SUBP * 8, 256)
            prod = jnp.dot(rows, mc_ref[:, 256:512], preferred_element_type=f32)
            for q in range(2):
                u[q, 0] = prod[:, 128 * q : 128 * q + 128]
            for q in range(2):
                edges[(here + 1) % NZ, q] = u[q, 0, pl.ds(0, SUBP, stride=8), :]

        edge[...] = edges[here + 1]

        def both(g, carry):
            granule(i, g)
            return carry

        lax.fori_loop(0, 2, both, 0)
        edges[here] = edge[...]
        exchange(i).start()

    edges[NZ] = jnp.zeros((2, SUBP, 128), f32)
    compress(0)

    a_copy.wait()
    for ref, low, count in ((ay, 0, BY), (az, BY, BZ)):
        for part in range(2):
            rows = slice(128 * part + low, 128 * part + low + count)
            mine, other = a_ref[rows], aoth[rows]
            ref[part * count : (part + 1) * count, 0:128] = mine
            ref[part * count : (part + 1) * count, 128:256] = other
            ref[(2 + part) * count : (3 + part) * count, 0:128] = mine
            ref[(2 + part) * count : (3 + part) * count, 128:256] = -other

    rby[:, 12] = jnp.zeros((2, BY, WIDE), bf16)
    rbz[:, 14] = jnp.zeros((2, BZ, WIDE), bf16)
    for d in range(2):
        unsent = slice(COLS, WIDE) if d == 0 else slice(0, COLS)
        rb2[d, 0, :, unsent] = jnp.zeros((BY, COLS), bf16)
        rb3[d, 0, :, unsent] = jnp.zeros((BZ, COLS), bf16)

    def partial_image(ref, low, count, tile, adds, put):
        par = tile % 2
        beams = slice(low, low + count)
        for at in range(0, COLS, 256):
            cols = slice(at, at + 256)
            imag = slice(COLS + at, COLS + at + 256)
            data = xb[tile, 0:2, :, cols].reshape(256, 256)
            r = jnp.dot(ref[...], data, preferred_element_type=f32)
            c, s = d0_ref[0, par, beams, cols], d0_ref[1, par, beams, cols]
            re = c * r[0:count] - s * r[3 * count :]
            im = c * r[count : 2 * count] + s * r[2 * count : 3 * count]
            for got in adds:
                re = re + got[:, cols].astype(f32)
                im = im + got[:, imag].astype(f32)
            put(cols, re)
            put(imag, im)

    def put_to(ref):
        def put(cols, value):
            ref[:, cols] = value.astype(ref.dtype)
        return put

    def y_to(d):
        return turn_at(z, y + 1 + 2 * d)

    def z_to(d):
        return turn_at(z + 1 + (NZ - 2) * d, y)

    def y_copy(d, k):
        return remote(sby.at[d, k], rby.at[d, k], y_s.at[d, k], y_r.at[d, k], {"turn": y_to(d)})

    def z_copy(d, k):
        return remote(sbz.at[d, k], rbz.at[d, k], z_s.at[d, k], z_r.at[d, k], {"turn": z_to(d)})

    def y_message(c, near, d):
        k = jnp.where(near == 1, 4 + c, c // 2)
        takes = (near == 1) & (c % 2 == d)
        src = jnp.where(takes, c // 2, 12)

        @pl.when(takes)
        def _():
            y_copy(d, c // 2).wait_recv()

        tile = turn_at(chunk(c), y + 2 + near * (2 * d - 1))
        partial_image(ay, 0, BY, tile, (rby.at[d, src],), put_to(sby.at[d, k]))
        y_copy(d, k).start()

    def z_far(d, j):
        tile = turn_at(chunk(0), y + order(j + 2 * d, NY))
        partial_image(az, BY, BZ, tile, (), put_to(sbz.at[d, j]))
        z_copy(d, j).start()

    def z_near(c, j):
        d = (c + 1) % 2
        step = (c - 1) // 2
        k = 2 + 4 * step + j
        takes = (step > 0) | (j // 2 == d)
        prev = jnp.where(step > 0, k - 4, j - 2 * d)
        src = jnp.where(takes, prev, 14)

        @pl.when(takes)
        def _():
            z_copy(d, prev).wait_recv()

        tile = turn_at(chunk(c), y + order(j, NY))
        partial_image(az, BY, BZ, tile, (rbz.at[d, src],), put_to(sbz.at[d, k]))
        z_copy(d, k).start()

    halves = (slice(0, COLS), slice(COLS, WIDE))

    def far2(d):
        part = halves[d]
        return remote(sb2.at[d, 0, :, part], rb2.at[d, 0, :, part], s2_s.at[d, 0], s2_r.at[d, 0], {"turn": z_to(d)})

    def near2(d, k):
        return remote(sb2.at[d, k], rb2.at[d, k], s2_s.at[d, k], s2_r.at[d, k], {"turn": z_to(d)})

    def far3(d):
        part = halves[d]
        return remote(sb3.at[d, 0, :, part], rb3.at[d, 0, :, part], s3_s.at[d, 0], s3_r.at[d, 0], {"turn": y_to(d)})

    def near3(d, k):
        return remote(sb3.at[d, k], rb3.at[d, k], s3_s.at[d, k], s3_r.at[d, k], {"turn": y_to(d)})

    def wait_y(i):
        for d in range(2):
            y_copy(d, 4 + i).wait_recv()
        return (rby.at[0, 4 + i], rby.at[1, 4 + i])

    def wait_z(i):
        for d in range(2):
            z_copy(d, 10 + i).wait_recv()
        return (rbz.at[0, 10 + i], rbz.at[1, 10 + i])

    def put_both(ref):
        def put(cols, value):
            d = 0 if cols.start < COLS else 1
            ref[d, 0, :, cols] = value.astype(bf16)
        return put

    def second_far():
        partial_image(ay, 0, BY, turn_at(z + 4, y), wait_y(0), put_both(sb2))
        for d in range(2):
            far2(d).start()

    def second_y(i):
        d = (i + 1) % 2
        q = (i - 1) // 2
        adds = wait_y(i)
        for side in range(2):
            @pl.when((q == 0) & (d == side))
            def _():
                far2(side).wait_recv()

        @pl.when(q > 0)
        def _():
            near2(d, q).wait_recv()

        partial_image(ay, 0, BY, turn_at(chunk(i), y), adds + (rb2.at[d, q],), put_to(sb2.at[d, q + 1]))
        near2(d, q + 1).start()

    def second_z(i):
        adds = wait_z(i)
        tile = turn_at(z, y + (2, 1, 3, 0)[i])
        if i == 0:
            partial_image(az, BY, BZ, tile, adds, put_both(sb3))
            for d in range(2):
                far3(d).start()
        elif i < 3:
            d = i - 1
            far3(d).wait_recv()
            partial_image(az, BY, BZ, tile, adds + (rb3.at[d, 0],), put_to(sb3.at[d, 1]))
            near3(d, 1).start()
        else:
            for d in range(2):
                near3(d, 1).wait_recv()
            adds = adds + (rb3.at[0, 1], rb3.at[1, 1])
            partial_image(az, BY, BZ, tile, adds, put_to(img.at[pl.ds(BY, BZ)]))

    def main_loop(i, carry):
        @pl.when(i < NZ)
        def _():
            compress(i)

        @pl.when(i <= NZ)
        def _():
            c = i - 1
            exchange(c).wait_recv()

            def pair(near, carry):
                y_message(c, near, (c + near) % 2)
                return carry

            lax.fori_loop(0, jnp.where(c < 4, 2, 1), pair, 0)

        @pl.when(i == 1)
        def _():
            def far(n, carry):
                z_far(n // 2, n % 2)
                return carry

            lax.fori_loop(0, 4, far, 0)

        @pl.when((i >= 3) & (i <= NZ))
        def _():
            def near(j, carry):
                z_near(i - 2, j)
                return carry

            lax.fori_loop(0, 4, near, 0)

        @pl.when(i >= 4)
        def _():
            def pair(n, carry):
                y_message(i - 4, 1, (i + n) % 2)
                return carry

            lax.fori_loop(0, jnp.where(i < 8, 1, 2), pair, 0)

        @pl.when(i == NZ)
        def _():
            second_far()

        @pl.when(i > NZ)
        def _():
            second_y(i - NZ)

        return carry

    lax.fori_loop(1, 12, main_loop, 0)

    def second_loop(i, carry):
        second_y(i)
        return carry

    beam = iota((BEAMS, 128), 0)
    odd = 2 * beam + 1 - BEAMS
    bins = iota((BEAMS, 128), 1) + 1 + COLS * core + 2 * COLS * turn
    for level in (1, 2):
        side = (leaf >> level) % 2
        i12[level - 1] = interp(taps_ref[level, side])
        rate = odd * ((2 * side - 1) * (level + 2))
        blocks = phase_blocks(rate * bins + beam * beam * (side + 1), rate * 128, COLS // 128)
        for b, (c, s) in enumerate(blocks):
            at = slice(128 * b, 128 * b + 128)
            d12[level - 1, 0, :, at] = c
            d12[level - 1, 1, :, at] = s

    second_z(0)
    lax.fori_loop(4, 5, second_loop, 0)
    second_z(1)
    second_z(2)
    lax.fori_loop(5, 7, second_loop, 0)
    second_z(3)
    adds = wait_y(7)
    for d in range(2):
        near2(d, 3).wait_recv()
    partial_image(ay, 0, BY, turn, adds + (rb2.at[0, 3], rb2.at[1, 3]), put_to(img.at[pl.ds(0, BY)]))

    for level in range(2):
        value = img[...]
        high = value.astype(bf16)
        low = (value - high.astype(f32)).astype(bf16)
        matrix = i12[level]
        moved = jnp.dot(matrix, high, preferred_element_type=f32) + jnp.dot(matrix, low, preferred_element_type=f32)
        c, s = d12[level, 0], d12[level, 1]
        re = c * moved[:, :COLS] - s * moved[:, COLS:]
        im = c * moved[:, COLS:] + s * moved[:, :COLS]
        target = img if level == 0 else vout
        target[:, :COLS] = re.astype(target.dtype)
        target[:, COLS:] = im.astype(target.dtype)

    def share(e):
        to = (leaf + e) % NLEAF
        rows = pl.ds(pl.multiple_of(16 * to, 16), 16)
        return remote(vout.at[rows], rl.at[leaf], l_s.at[e - 1], l_r.at[e - 1], {"leaf": to})

    def shared(e):
        src = (leaf + NLEAF - e) % NLEAF
        return remote(vout.at[pl.ds(0, 16)], rl.at[src], l_s.at[e - 1], l_r.at[e - 1], {"leaf": mate})

    for e in range(1, NLEAF):
        share(e).start()
    rl[leaf] = vout[pl.ds(pl.multiple_of(16 * leaf, 16), 16)]
    for e in range(1, NLEAF):
        shared(e).wait_recv()
    for side in range(2):
        total = rl[side].astype(f32)
        for xx in range(1, 4):
            total = total + rl[2 * xx + side].astype(f32)
        total = total.astype(bf16)
        for b in range(4):
            out_ref[4 * side + b, :, 0:128] = total[:, 128 * b : 128 * b + 128]
            out_ref[4 * side + b, :, 128:256] = total[:, COLS + 128 * b : COLS + 128 * b + 128]

    def sent_y(k, carry):
        for d in range(2):
            y_copy(d, k).wait_send()
        return carry

    def sent_z(k, carry):
        for d in range(2):
            z_copy(d, k).wait_send()
        return carry

    def sent_mate(i, carry):
        exchange(i).wait_send()
        return carry

    lax.fori_loop(0, NZ, sent_mate, 0)
    lax.fori_loop(0, 12, sent_y, 0)
    lax.fori_loop(0, 14, sent_z, 0)
    for d in range(2):
        far2(d).wait_send()
        far3(d).wait_send()
        near3(d, 1).wait_send()
        for k in range(1, 4):
            near2(d, k).wait_send()
    for e in range(1, NLEAF):
        share(e).wait_send()


def reduce_merge(x, mc, a, d0, taps):
    vmem = pl.BlockSpec(memory_space=pltpu.VMEM)
    dma = pltpu.SemaphoreType.DMA
    return pl.pallas_call(
        main_kernel,
        out_shape=jax.ShapeDtypeStruct((8, 16, 256), bf16),
        in_specs=[pl.BlockSpec(memory_space=pl.ANY)] + [vmem] * 4,
        out_specs=vmem,
        scratch_shapes=[
            pltpu.VMEM((2, 2, SUBP, GRAN, 256), bf16),
            pltpu.VMEM((2, SUBP, 8, 256), bf16),
            pltpu.VMEM((4, 2, SUBP * 8, 128), f32),
            pltpu.VMEM((2, SUBP, 128), f32),
            pltpu.VMEM((NZ + 1, 2, SUBP, 128), f32),
            pltpu.VMEM((TILES, 3, 128, COLS), bf16),
            pltpu.VMEM((256, 128), bf16),
            pltpu.VMEM((4 * BY, 256), bf16),
            pltpu.VMEM((4 * BZ, 256), bf16),
            pltpu.VMEM((2, 13, BY, WIDE), bf16),
            pltpu.VMEM((2, 12, BY, WIDE), bf16),
            pltpu.VMEM((2, 15, BZ, WIDE), bf16),
            pltpu.VMEM((2, 14, BZ, WIDE), bf16),
            pltpu.VMEM((2, 4, BY, WIDE), bf16),
            pltpu.VMEM((2, 4, BY, WIDE), bf16),
            pltpu.VMEM((2, 2, BZ, WIDE), bf16),
            pltpu.VMEM((2, 2, BZ, WIDE), bf16),
            pltpu.VMEM((BEAMS, WIDE), f32),
            pltpu.VMEM((BEAMS, WIDE), bf16),
            pltpu.VMEM((NLEAF, 16, WIDE), bf16),
            pltpu.VMEM((2, BEAMS, BEAMS), bf16),
            pltpu.VMEM((2, 2, BEAMS, COLS), f32),
            dma((2, 2)), dma((2,)), dma((NZ,)), dma((NZ,)), dma, dma,
            dma((2, 12)), dma((2, 12)), dma((2, 14)), dma((2, 14)),
            dma((2, 4)), dma((2, 4)), dma((2, 2)), dma((2, 2)),
            dma((NLEAF - 1,)), dma((NLEAF - 1,)),
        ],
        compiler_params=pltpu.CompilerParams(
            collective_id=0, has_side_effects=True, vmem_limit_bytes=60 * 1024 * 1024
        ),
        name="reduce_merge",
    )(x, mc, a, d0, taps)


def per_device(echoes, chirp, taps, slots):
    taps = jnp.transpose(taps, (0, 1, 3, 2))
    tables = prepare(chirp, taps, slots)
    image = reduce_merge(echoes, *tables, taps)
    return jnp.transpose(image, (1, 0, 2))


def solution(mesh):
    placed = (P(("leaf", "turn"), None, None), P(), P(), P("leaf", None))
    return jax.shard_map(
        per_device, mesh=mesh, in_specs=placed, out_specs=P("leaf", "turn", None), check_vma=False
    )
```

```python
import functools
import math

import jax
import jax.numpy as jnp
from jax import lax
from jax.experimental import pallas as pl
from jax.experimental.pallas import tpu as pltpu
from jax.sharding import PartitionSpec as P

WEIGHTS = (-1.0 / 32, 3.0 / 32, -7.0 / 32, 21.0 / 32, 21.0 / 32, -7.0 / 32, 3.0 / 32, -1.0 / 32)
MESH = pl.DeviceIdType.MESH

BEAMS = 128
TAPS = 8
SUBP = 64
NSUB = 32
NZ = 8
NY = 4
NLEAF = 8
TILES = NZ * NY
COLS = 512
WIDE = 2 * COLS
BY = 80
BZ = BEAMS - BY
GRAN = 16
NGRAN = 256 // GRAN

f32 = jnp.float32
bf16 = jnp.bfloat16


def cos_sin(n):
    n = n & 4095
    quad = (n + 512) >> 10
    m = (n - (quad << 10)).astype(f32) * (2.0 * math.pi / 4096)
    m2 = m * m
    s = m * (1.0 + m2 * (-1.0 / 6 + m2 * (1.0 / 120 + m2 * (-1.0 / 5040 + m2 * (1.0 / 362880)))))
    c = 1.0 + m2 * (-0.5 + m2 * (1.0 / 24 + m2 * (-1.0 / 720 + m2 * (1.0 / 40320))))
    odd = (quad & 1) == 1
    cc = jnp.where(odd, s, c)
    ss = jnp.where(odd, c, s)
    cos = jnp.where((quad == 1) | (quad == 2), -cc, cc)
    sin = jnp.where((quad == 2) | (quad == 3), -ss, ss)
    return cos, sin


def iota(shape, dim):
    return lax.broadcasted_iota(jnp.int32, shape, dim)


def interp(rows):
    cells = iota((BEAMS, BEAMS), 0)
    total = jnp.zeros((BEAMS, BEAMS), f32)
    for t in range(TAPS):
        total = total + jnp.where(rows[t : t + 1, :] == cells, WEIGHTS[t], 0.0)
    return total.T.astype(bf16)


def phase_blocks(first, step, count):
    c, s = cos_sin(first)
    blocks = [(c, s)]
    fc, fs = cos_sin(step)
    for _ in range(count - 1):
        c, s = c * fc - s * fs, s * fc + c * fs
        blocks.append((c, s))
    return blocks


def first_tables(chirp_ref, taps_ref, slots_ref, mc_ref, a_ref, d0_ref):
    leaf = lax.axis_index("leaf")
    turn = lax.axis_index("turn")
    core = leaf % 2
    sq = (BEAMS, BEAMS)

    g = jnp.broadcast_to(chirp_ref[...][:, None, :], (2, 8, 128)).reshape(16, 128)
    flip = ((iota(sq, 0) + iota(sq, 1)) % 128 == 0).astype(bf16)
    h = jnp.dot(g, flip, preferred_element_type=f32)
    lower = iota(sq, 0) >= iota(sq, 1)
    tabs = []
    for part in range(2):
        row = jnp.broadcast_to(h[8 * part : 8 * part + 1], sq)
        tabs.append(pltpu.roll(row, 0, 1, stride=1, stride_axis=0))
    for side in range(2):
        re, im = (jnp.where(lower if side == 0 else ~lower, t, 0.0) for t in tabs)
        at = 256 * side
        mc_ref[0:128, at : at + 128] = re.astype(bf16)
        mc_ref[0:128, at + 128 : at + 256] = im.astype(bf16)
        mc_ref[128:256, at : at + 128] = (-im).astype(bf16)
        mc_ref[128:256, at + 128 : at + 256] = re.astype(bf16)

    slot = slots_ref[0, turn]
    beam = iota(sq, 0)
    lane = iota(sq, 1)
    m = lane % SUBP
    n = (2 * beam + 1 - BEAMS) * (2 * m + 1 - SUBP) + 3 * (beam + 1) * (2 * slot + 1) * (2 * m + 1)
    cos, sin = cos_sin(8 * n)
    scale = 1.0 / math.sqrt(2.0 * NSUB * SUBP)
    cos, sin = cos * scale, sin * scale
    first = lane < SUBP
    s_re = jnp.where(first, cos, -sin).astype(bf16)
    s_im = jnp.where(first, sin, cos).astype(bf16)
    i0 = interp(taps_ref[0, core])
    z_re = jnp.dot(i0, s_re, preferred_element_type=f32)
    z_im = jnp.dot(i0, s_im, preferred_element_type=f32)
    ca, sa = cos_sin(beam * beam * (core + 1))
    a_ref[0:128] = (ca * z_re - sa * z_im).astype(bf16)
    a_ref[128:256] = (ca * z_im + sa * z_re).astype(bf16)

    odd = 2 * beam + 1 - BEAMS
    sign = (2 * core - 1).astype(f32)
    blocks = phase_blocks(2 * odd * (lane + COLS * core + 1), 2 * odd * 128, COLS // 128)
    for b, (c, s) in enumerate(blocks):
        at = slice(128 * b, 128 * b + 128)
        d0_ref[0, 0, :, at] = c
        d0_ref[0, 1, :, at] = -c
        d0_ref[1, 0, :, at] = s * sign
        d0_ref[1, 1, :, at] = -s * sign


def main_kernel(
    x_ref, chirp_ref, taps_ref, slots_ref, out_ref,
    xbuf, ebuf, u, edge, edges, xb, aoth, ay, az,
    rby, sby, rbz, sbz, rb2, sb2, rb3, sb3, img, vout, rl, i12, d12, mc_ref, a_ref, d0_ref,
    in_sem, e_sem, ex_s, ex_r, a_s, a_r, y_s, y_r, z_s, z_r, s2_s, s2_r, s3_s, s3_r, l_s, l_r,
):
    leaf = lax.axis_index("leaf")
    turn = lax.axis_index("turn")
    core = leaf % 2
    z = turn // NY
    y = turn % NY
    mate = leaf + 1 - 2 * core

    def turn_at(zz, yy):
        return (zz % NZ) * NY + yy % NY

    ynbr = (turn_at(z, y + 1), turn_at(z, y + NY - 1))
    znbr = (turn_at(z + 1, y), turn_at(z + NZ - 1, y))

    def order(i, n):
        step = (i + 1) // 2
        return n // 2 + (1 - 2 * (i % 2)) * step

    def chunk(i):
        return (z + order(i, NZ)) % NZ

    def pull(i, g):
        at = pl.multiple_of((2 * chunk(i) + 1 - g) * GRAN, GRAN)
        return pltpu.make_async_copy(x_ref.at[:, pl.ds(at, GRAN), :], xbuf.at[i % 2, g], in_sem.at[i % 2, g])

    def pull_edge(i):
        at = pl.multiple_of((chunk(i) + 1) % NZ * 2 * GRAN, 8)
        slot = i // 2 % 2
        return pltpu.make_async_copy(x_ref.at[:, pl.ds(at, 8), :], ebuf.at[slot], e_sem.at[slot])

    pull_edge(0).start()
    for g in range(2):
        pull(0, g).start()

    barrier = pltpu.get_barrier_semaphore()
    for t in ynbr + znbr:
        pl.semaphore_signal(barrier, inc=1, device_id={"turn": t}, device_id_type=MESH)
    for e in range(1, NLEAF):
        pl.semaphore_signal(barrier, inc=1, device_id={"leaf": (leaf + e) % NLEAF}, device_id_type=MESH)
    first_tables(chirp_ref, taps_ref, slots_ref, mc_ref, a_ref, d0_ref)

    def remote(src, dst, ssem, rsem, where):
        return pltpu.make_async_remote_copy(
            src_ref=src, dst_ref=dst, send_sem=ssem, recv_sem=rsem,
            device_id=where, device_id_type=MESH,
        )

    a_copy = remote(a_ref, aoth, a_s, a_r, {"leaf": mate})

    def exchange(i):
        four = pl.ds(4 * chunk(i), 4)
        return remote(xb.at[four, 2], xb.at[four, 1], ex_s.at[i], ex_r.at[i], {"leaf": mate})

    def granule(i, g):
        pull(i, g).wait()
        gi = 2 * chunk(i) + 1 - g
        for hf in range(2):
            rows = xbuf[i % 2, g, pl.ds(32 * hf, 32)].reshape(32 * GRAN, 256)
            prod = jnp.dot(rows, mc_ref[...], preferred_element_type=f32).reshape(32, 2, 8, 512)
            for q in range(4):
                for e in range(2):
                    part = prod[:, e, :, 128 * q : 128 * q + 128].reshape(256, 128)
                    u[q, e, 256 * hf : 256 * hf + 256, :] = part
        for b in range(GRAN):
            half = b % 8 // 4
            plane = 2 * (core if half == 0 else 1 - core)
            tile = 2 * gi + b // 8
            at = 128 * (b % 4)
            for q in range(2):
                own = u[q, b // 8, pl.ds(b % 8, SUBP, stride=8), :]
                if b == GRAN - 1:
                    nxt = edge[q]
                else:
                    nxt = u[2 + q, (b + 1) // 8, pl.ds((b + 1) % 8, SUBP, stride=8), :]
                xb[tile, plane, 64 * q : 64 * q + 64, at : at + 128] = (own + nxt).astype(bf16)
        for q in range(2):
            edge[q] = u[2 + q, 0, pl.ds(0, SUBP, stride=8), :]

    def compress(i):
        @pl.when(i + 1 < NZ)
        def _():
            for g in range(2):
                pull(i + 1, g).start()

        @pl.when((i % 2 == 1) & (i + 1 < NZ))
        def _():
            pull_edge(i + 1).start()

        here = chunk(i)

        @pl.when(i % 2 == 0)
        def _():
            pull_edge(i).wait()
            rows = ebuf[i // 2 % 2].reshape(SUBP * 8, 256)
            prod = jnp.dot(rows, mc_ref[:, 256:512], preferred_element_type=f32)
            for q in range(2):
                u[q, 0] = prod[:, 128 * q : 128 * q + 128]
            for q in range(2):
                edges[(here + 1) % NZ, q] = u[q, 0, pl.ds(0, SUBP, stride=8), :]

        edge[...] = edges[here + 1]

        def both(g, carry):
            granule(i, g)
            return carry

        lax.fori_loop(0, 2, both, 0)
        edges[here] = edge[...]

    rby[:, 12] = jnp.zeros((2, BY, WIDE), bf16)
    rbz[:, 14] = jnp.zeros((2, BZ, WIDE), bf16)
    for d in range(2):
        unsent = slice(COLS, WIDE) if d == 0 else slice(0, COLS)
        rb2[d, 0, :, unsent] = jnp.zeros((BY, COLS), bf16)
        rb3[d, 0, :, unsent] = jnp.zeros((BZ, COLS), bf16)
    edges[NZ] = jnp.zeros((2, SUBP, 128), f32)
    compress(0)
    pl.semaphore_wait(barrier, 4 + NLEAF - 1)
    a_copy.start()
    exchange(0).start()

    a_copy.wait()
    for ref, low, count in ((ay, 0, BY), (az, BY, BZ)):
        for part in range(2):
            rows = slice(128 * part + low, 128 * part + low + count)
            mine, other = a_ref[rows], aoth[rows]
            ref[part * count : (part + 1) * count, 0:128] = mine
            ref[part * count : (part + 1) * count, 128:256] = other
            ref[(2 + part) * count : (3 + part) * count, 0:128] = mine
            ref[(2 + part) * count : (3 + part) * count, 128:256] = -other

    def partial_image(ref, low, count, tile, adds, put):
        par = tile % 2
        beams = slice(low, low + count)
        for at in range(0, COLS, 256):
            cols = slice(at, at + 256)
            imag = slice(COLS + at, COLS + at + 256)
            data = xb[tile, 0:2, :, cols].reshape(256, 256)
            r = jnp.dot(ref[...], data, preferred_element_type=f32)
            c, s = d0_ref[0, par, beams, cols], d0_ref[1, par, beams, cols]
            re = c * r[0:count] - s * r[3 * count :]
            im = c * r[count : 2 * count] + s * r[2 * count : 3 * count]
            for got in adds:
                re = re + got[:, cols].astype(f32)
                im = im + got[:, imag].astype(f32)
            put(cols, re)
            put(imag, im)

    def put_to(ref):
        def put(cols, value):
            ref[:, cols] = value.astype(ref.dtype)
        return put

    def y_to(d):
        return turn_at(z, y + 1 + 2 * d)

    def z_to(d):
        return turn_at(z + 1 + (NZ - 2) * d, y)

    def y_copy(d, k):
        return remote(sby.at[d, k], rby.at[d, k], y_s.at[d, k], y_r.at[d, k], {"turn": y_to(d)})

    def z_copy(d, k):
        return remote(sbz.at[d, k], rbz.at[d, k], z_s.at[d, k], z_r.at[d, k], {"turn": z_to(d)})

    def y_message(c, near, d):
        k = jnp.where(near == 1, 4 + c, c // 2)
        takes = (near == 1) & (c % 2 == d)
        src = jnp.where(takes, c // 2, 12)

        @pl.when(takes)
        def _():
            y_copy(d, c // 2).wait_recv()

        tile = turn_at(chunk(c), y + 2 + near * (2 * d - 1))
        partial_image(ay, 0, BY, tile, (rby.at[d, src],), put_to(sby.at[d, k]))
        y_copy(d, k).start()

    def z_far(d, j):
        tile = turn_at(chunk(0), y + order(j + 2 * d, NY))
        partial_image(az, BY, BZ, tile, (), put_to(sbz.at[d, j]))
        z_copy(d, j).start()

    def z_near(c, j):
        d = (c + 1) % 2
        step = (c - 1) // 2
        k = 2 + 4 * step + j
        takes = (step > 0) | (j // 2 == d)
        prev = jnp.where(step > 0, k - 4, j - 2 * d)
        src = jnp.where(takes, prev, 14)

        @pl.when(takes)
        def _():
            z_copy(d, prev).wait_recv()

        tile = turn_at(chunk(c), y + order(j, NY))
        partial_image(az, BY, BZ, tile, (rbz.at[d, src],), put_to(sbz.at[d, k]))
        z_copy(d, k).start()

    halves = (slice(0, COLS), slice(COLS, WIDE))

    def far2(d):
        part = halves[d]
        return remote(sb2.at[d, 0, :, part], rb2.at[d, 0, :, part], s2_s.at[d, 0], s2_r.at[d, 0], {"turn": z_to(d)})

    def near2(d, k):
        return remote(sb2.at[d, k], rb2.at[d, k], s2_s.at[d, k], s2_r.at[d, k], {"turn": z_to(d)})

    def far3(d):
        part = halves[d]
        return remote(sb3.at[d, 0, :, part], rb3.at[d, 0, :, part], s3_s.at[d, 0], s3_r.at[d, 0], {"turn": y_to(d)})

    def near3(d, k):
        return remote(sb3.at[d, k], rb3.at[d, k], s3_s.at[d, k], s3_r.at[d, k], {"turn": y_to(d)})

    def wait_y(i):
        for d in range(2):
            y_copy(d, 4 + i).wait_recv()
        return (rby.at[0, 4 + i], rby.at[1, 4 + i])

    def wait_z(i):
        for d in range(2):
            z_copy(d, 10 + i).wait_recv()
        return (rbz.at[0, 10 + i], rbz.at[1, 10 + i])

    def put_both(ref):
        def put(cols, value):
            d = 0 if cols.start < COLS else 1
            ref[d, 0, :, cols] = value.astype(bf16)
        return put

    def second_far():
        partial_image(ay, 0, BY, turn_at(z + 4, y), wait_y(0), put_both(sb2))
        for d in range(2):
            far2(d).start()

    def second_y(i):
        d = (i + 1) % 2
        q = (i - 1) // 2
        adds = wait_y(i)
        for side in range(2):
            @pl.when((q == 0) & (d == side))
            def _():
                far2(side).wait_recv()

        @pl.when(q > 0)
        def _():
            near2(d, q).wait_recv()

        partial_image(ay, 0, BY, turn_at(chunk(i), y), adds + (rb2.at[d, q],), put_to(sb2.at[d, q + 1]))
        near2(d, q + 1).start()

    def second_z(i):
        adds = wait_z(i)
        tile = turn_at(z, y + (2, 1, 3, 0)[i])
        if i == 0:
            partial_image(az, BY, BZ, tile, adds, put_both(sb3))
            for d in range(2):
                far3(d).start()
        elif i < 3:
            d = i - 1
            far3(d).wait_recv()
            partial_image(az, BY, BZ, tile, adds + (rb3.at[d, 0],), put_to(sb3.at[d, 1]))
            near3(d, 1).start()
        else:
            for d in range(2):
                near3(d, 1).wait_recv()
            adds = adds + (rb3.at[0, 1], rb3.at[1, 1])
            partial_image(az, BY, BZ, tile, adds, put_to(img.at[pl.ds(BY, BZ)]))

    def main_loop(i, carry):
        @pl.when(i < NZ)
        def _():
            compress(i)
            exchange(i).start()

        @pl.when(i <= NZ)
        def _():
            c = i - 1
            exchange(c).wait_recv()

            def pair(near, carry):
                y_message(c, near, (c + near) % 2)
                return carry

            lax.fori_loop(0, jnp.where(c < 4, 2, 1), pair, 0)

        @pl.when(i == 1)
        def _():
            def far(n, carry):
                z_far(n // 2, n % 2)
                return carry

            lax.fori_loop(0, 4, far, 0)

        @pl.when((i >= 3) & (i <= NZ))
        def _():
            def near(j, carry):
                z_near(i - 2, j)
                return carry

            lax.fori_loop(0, 4, near, 0)

        @pl.when(i >= 4)
        def _():
            def pair(n, carry):
                y_message(i - 4, 1, (i + n) % 2)
                return carry

            lax.fori_loop(0, jnp.where(i < 8, 1, 2), pair, 0)

        @pl.when(i == NZ)
        def _():
            second_far()

        @pl.when(i > NZ)
        def _():
            second_y(i - NZ)

        return carry

    lax.fori_loop(1, 12, main_loop, 0)

    def second_loop(i, carry):
        second_y(i)
        return carry

    beam = iota((BEAMS, 128), 0)
    odd = 2 * beam + 1 - BEAMS
    bins = iota((BEAMS, 128), 1) + 1 + COLS * core + 2 * COLS * turn
    for level in (1, 2):
        side = (leaf >> level) % 2
        i12[level - 1] = interp(taps_ref[level, side])
        rate = odd * ((2 * side - 1) * (level + 2))
        blocks = phase_blocks(rate * bins + beam * beam * (side + 1), rate * 128, COLS // 128)
        for b, (c, s) in enumerate(blocks):
            at = slice(128 * b, 128 * b + 128)
            d12[level - 1, 0, :, at] = c
            d12[level - 1, 1, :, at] = s

    second_z(0)
    lax.fori_loop(4, 5, second_loop, 0)
    second_z(1)
    second_z(2)
    lax.fori_loop(5, 7, second_loop, 0)
    second_z(3)
    adds = wait_y(7)
    for d in range(2):
        near2(d, 3).wait_recv()
    partial_image(ay, 0, BY, turn, adds + (rb2.at[0, 3], rb2.at[1, 3]), put_to(img.at[pl.ds(0, BY)]))

    for level in range(2):
        value = img[...]
        high = value.astype(bf16)
        low = (value - high.astype(f32)).astype(bf16)
        matrix = i12[level]
        moved = jnp.dot(matrix, high, preferred_element_type=f32) + jnp.dot(matrix, low, preferred_element_type=f32)
        c, s = d12[level, 0], d12[level, 1]
        re = c * moved[:, :COLS] - s * moved[:, COLS:]
        im = c * moved[:, COLS:] + s * moved[:, :COLS]
        target = img if level == 0 else vout
        target[:, :COLS] = re.astype(target.dtype)
        target[:, COLS:] = im.astype(target.dtype)

    def share(e):
        to = (leaf + e) % NLEAF
        rows = pl.ds(pl.multiple_of(16 * to, 16), 16)
        return remote(vout.at[rows], rl.at[leaf], l_s.at[e - 1], l_r.at[e - 1], {"leaf": to})

    def shared(e):
        src = (leaf + NLEAF - e) % NLEAF
        return remote(vout.at[pl.ds(0, 16)], rl.at[src], l_s.at[e - 1], l_r.at[e - 1], {"leaf": mate})

    for e in range(1, NLEAF):
        share(e).start()
    rl[leaf] = vout[pl.ds(pl.multiple_of(16 * leaf, 16), 16)]
    for e in range(1, NLEAF):
        shared(e).wait_recv()
    for side in range(2):
        total = rl[side].astype(f32)
        for xx in range(1, 4):
            total = total + rl[2 * xx + side].astype(f32)
        total = total.astype(bf16)
        for b in range(4):
            out_ref[4 * side + b, :, 0:128] = total[:, 128 * b : 128 * b + 128]
            out_ref[4 * side + b, :, 128:256] = total[:, COLS + 128 * b : COLS + 128 * b + 128]

    def sent_y(k, carry):
        for d in range(2):
            y_copy(d, k).wait_send()
        return carry

    def sent_z(k, carry):
        for d in range(2):
            z_copy(d, k).wait_send()
        return carry

    def sent_mate(i, carry):
        exchange(i).wait_send()
        return carry

    lax.fori_loop(0, NZ, sent_mate, 0)
    lax.fori_loop(0, 12, sent_y, 0)
    lax.fori_loop(0, 14, sent_z, 0)
    for d in range(2):
        far2(d).wait_send()
        far3(d).wait_send()
        near3(d, 1).wait_send()
        for k in range(1, 4):
            near2(d, k).wait_send()
    for e in range(1, NLEAF):
        share(e).wait_send()


def reduce_merge(x, chirp, taps, slots):
    vmem = pl.BlockSpec(memory_space=pltpu.VMEM)
    dma = pltpu.SemaphoreType.DMA
    return pl.pallas_call(
        main_kernel,
        out_shape=jax.ShapeDtypeStruct((8, 16, 256), bf16),
        in_specs=[pl.BlockSpec(memory_space=pl.ANY), vmem, vmem, pl.BlockSpec(memory_space=pltpu.SMEM)],
        out_specs=vmem,
        scratch_shapes=[
            pltpu.VMEM((2, 2, SUBP, GRAN, 256), bf16),
            pltpu.VMEM((2, SUBP, 8, 256), bf16),
            pltpu.VMEM((4, 2, SUBP * 8, 128), f32),
            pltpu.VMEM((2, SUBP, 128), f32),
            pltpu.VMEM((NZ + 1, 2, SUBP, 128), f32),
            pltpu.VMEM((TILES, 3, 128, COLS), bf16),
            pltpu.VMEM((256, 128), bf16),
            pltpu.VMEM((4 * BY, 256), bf16),
            pltpu.VMEM((4 * BZ, 256), bf16),
            pltpu.VMEM((2, 13, BY, WIDE), bf16),
            pltpu.VMEM((2, 12, BY, WIDE), bf16),
            pltpu.VMEM((2, 15, BZ, WIDE), bf16),
            pltpu.VMEM((2, 14, BZ, WIDE), bf16),
            pltpu.VMEM((2, 4, BY, WIDE), bf16),
            pltpu.VMEM((2, 4, BY, WIDE), bf16),
            pltpu.VMEM((2, 2, BZ, WIDE), bf16),
            pltpu.VMEM((2, 2, BZ, WIDE), bf16),
            pltpu.VMEM((BEAMS, WIDE), f32),
            pltpu.VMEM((BEAMS, WIDE), bf16),
            pltpu.VMEM((NLEAF, 16, WIDE), bf16),
            pltpu.VMEM((2, BEAMS, BEAMS), bf16),
            pltpu.VMEM((2, 2, BEAMS, COLS), f32),
            pltpu.VMEM((256, 512), bf16),
            pltpu.VMEM((256, 128), bf16),
            pltpu.VMEM((2, 2, BEAMS, COLS), f32),
            dma((2, 2)), dma((2,)), dma((NZ,)), dma((NZ,)), dma, dma,
            dma((2, 12)), dma((2, 12)), dma((2, 14)), dma((2, 14)),
            dma((2, 4)), dma((2, 4)), dma((2, 2)), dma((2, 2)),
            dma((NLEAF - 1,)), dma((NLEAF - 1,)),
        ],
        compiler_params=pltpu.CompilerParams(
            collective_id=0, has_side_effects=True, vmem_limit_bytes=60 * 1024 * 1024
        ),
        name="reduce_merge",
    )(x, chirp, taps, slots)


def per_device(echoes, chirp, taps, slots):
    taps = jnp.transpose(taps, (0, 1, 3, 2))
    image = reduce_merge(echoes, chirp, taps, slots)
    return jnp.transpose(image, (1, 0, 2))


def solution(mesh):
    placed = (P(("leaf", "turn"), None, None), P(), P(), P("leaf", None))
    return jax.shard_map(
        per_device, mesh=mesh, in_specs=placed, out_specs=P("leaf", "turn", None), check_vma=False
    )
```

```python
import functools
import math

import jax
import jax.numpy as jnp
from jax import lax
from jax.experimental import pallas as pl
from jax.experimental.pallas import tpu as pltpu
from jax.sharding import PartitionSpec as P

WEIGHTS = (-1.0 / 32, 3.0 / 32, -7.0 / 32, 21.0 / 32, 21.0 / 32, -7.0 / 32, 3.0 / 32, -1.0 / 32)
MESH = pl.DeviceIdType.MESH

BEAMS = 128
TAPS = 8
SUBP = 64
NSUB = 32
NZ = 8
NY = 4
NLEAF = 8
TILES = NZ * NY
COLS = 512
WIDE = 2 * COLS
BY = 80
BZ = BEAMS - BY
GRAN = 16
NGRAN = 256 // GRAN

f32 = jnp.float32
bf16 = jnp.bfloat16


def cos_sin(n):
    n = n & 4095
    quad = (n + 512) >> 10
    m = (n - (quad << 10)).astype(f32) * (2.0 * math.pi / 4096)
    m2 = m * m
    s = m * (1.0 + m2 * (-1.0 / 6 + m2 * (1.0 / 120 + m2 * (-1.0 / 5040 + m2 * (1.0 / 362880)))))
    c = 1.0 + m2 * (-0.5 + m2 * (1.0 / 24 + m2 * (-1.0 / 720 + m2 * (1.0 / 40320))))
    odd = (quad & 1) == 1
    cc = jnp.where(odd, s, c)
    ss = jnp.where(odd, c, s)
    cos = jnp.where((quad == 1) | (quad == 2), -cc, cc)
    sin = jnp.where((quad == 2) | (quad == 3), -ss, ss)
    return cos, sin


def iota(shape, dim):
    return lax.broadcasted_iota(jnp.int32, shape, dim)


def interp(rows):
    cells = iota((BEAMS, BEAMS), 0)
    total = jnp.zeros((BEAMS, BEAMS), f32)
    for t in range(TAPS):
        total = total + jnp.where(rows[t : t + 1, :] == cells, WEIGHTS[t], 0.0)
    return total.T.astype(bf16)


def phase_blocks(first, step, count):
    c, s = cos_sin(first)
    blocks = [(c, s)]
    fc, fs = cos_sin(step)
    for _ in range(count - 1):
        c, s = c * fc - s * fs, s * fc + c * fs
        blocks.append((c, s))
    return blocks


def first_tables(chirp_ref, taps_ref, slots_ref, mc_ref, a_ref, d0_ref):
    leaf = lax.axis_index("leaf")
    turn = lax.axis_index("turn")
    core = leaf % 2
    sq = (BEAMS, BEAMS)

    g = jnp.broadcast_to(chirp_ref[...][:, None, :], (2, 8, 128)).reshape(16, 128)
    flip = ((iota(sq, 0) + iota(sq, 1)) % 128 == 0).astype(bf16)
    h = jnp.dot(g, flip, preferred_element_type=f32)
    lower = iota(sq, 0) >= iota(sq, 1)
    tabs = []
    for part in range(2):
        row = jnp.broadcast_to(h[8 * part : 8 * part + 1], sq)
        tabs.append(pltpu.roll(row, 0, 1, stride=1, stride_axis=0))
    for side in range(2):
        re, im = (jnp.where(lower if side == 0 else ~lower, t, 0.0) for t in tabs)
        at = 256 * side
        mc_ref[0:128, at : at + 128] = re.astype(bf16)
        mc_ref[0:128, at + 128 : at + 256] = im.astype(bf16)
        mc_ref[128:256, at : at + 128] = (-im).astype(bf16)
        mc_ref[128:256, at + 128 : at + 256] = re.astype(bf16)

    slot = slots_ref[0, turn]
    beam = iota(sq, 0)
    lane = iota(sq, 1)
    m = lane % SUBP
    n = (2 * beam + 1 - BEAMS) * (2 * m + 1 - SUBP) + 3 * (beam + 1) * (2 * slot + 1) * (2 * m + 1)
    cos, sin = cos_sin(8 * n)
    scale = 1.0 / math.sqrt(2.0 * NSUB * SUBP)
    cos, sin = cos * scale, sin * scale
    first = lane < SUBP
    s_re = jnp.where(first, cos, -sin).astype(bf16)
    s_im = jnp.where(first, sin, cos).astype(bf16)
    i0 = interp(taps_ref[0, core])
    z_re = jnp.dot(i0, s_re, preferred_element_type=f32)
    z_im = jnp.dot(i0, s_im, preferred_element_type=f32)
    ca, sa = cos_sin(beam * beam * (core + 1))
    a_ref[0:128] = (ca * z_re - sa * z_im).astype(bf16)
    a_ref[128:256] = (ca * z_im + sa * z_re).astype(bf16)

    odd = 2 * beam + 1 - BEAMS
    sign = (2 * core - 1).astype(f32)
    blocks = phase_blocks(2 * odd * (lane + COLS * core + 1), 2 * odd * 128, COLS // 128)
    for b, (c, s) in enumerate(blocks):
        at = slice(128 * b, 128 * b + 128)
        d0_ref[0, 0, :, at] = c
        d0_ref[0, 1, :, at] = -c
        d0_ref[1, 0, :, at] = s * sign
        d0_ref[1, 1, :, at] = -s * sign


def main_kernel(
    x_ref, chirp_ref, taps_ref, slots_ref, out_ref,
    xbuf, ebuf, u, edge, edges, xb, aoth, ay, az,
    rby, sby, rbz, sbz, rb2, sb2, rb3, sb3, img, vout, rl, i12, d12, mc_ref, a_ref, d0_ref,
    in_sem, e_sem, ex_s, ex_r, a_s, a_r, y_s, y_r, z_s, z_r, s2_s, s2_r, s3_s, s3_r, l_s, l_r,
):
    leaf = lax.axis_index("leaf")
    turn = lax.axis_index("turn")
    core = leaf % 2
    z = turn // NY
    y = turn % NY
    mate = leaf + 1 - 2 * core

    def turn_at(zz, yy):
        return (zz % NZ) * NY + yy % NY

    ynbr = (turn_at(z, y + 1), turn_at(z, y + NY - 1))
    znbr = (turn_at(z + 1, y), turn_at(z + NZ - 1, y))

    def order(i, n):
        step = (i + 1) // 2
        return n // 2 + (1 - 2 * (i % 2)) * step

    def chunk(i):
        return (z + order(i, NZ)) % NZ

    def pull(i, g):
        at = pl.multiple_of((2 * chunk(i) + 1 - g) * GRAN, GRAN)
        return pltpu.make_async_copy(x_ref.at[:, pl.ds(at, GRAN), :], xbuf.at[i % 2, g], in_sem.at[i % 2, g])

    def pull_edge(i):
        at = pl.multiple_of((chunk(i) + 1) % NZ * 2 * GRAN, 8)
        slot = i // 2 % 2
        return pltpu.make_async_copy(x_ref.at[:, pl.ds(at, 8), :], ebuf.at[slot], e_sem.at[slot])

    pull_edge(0).start()
    for g in range(2):
        pull(0, g).start()

    barrier = pltpu.get_barrier_semaphore()
    for t in ynbr + znbr:
        pl.semaphore_signal(barrier, inc=1, device_id={"turn": t}, device_id_type=MESH)
    for e in range(1, NLEAF):
        pl.semaphore_signal(barrier, inc=1, device_id={"leaf": (leaf + e) % NLEAF}, device_id_type=MESH)
    first_tables(chirp_ref, taps_ref, slots_ref, mc_ref, a_ref, d0_ref)

    def remote(src, dst, ssem, rsem, where):
        return pltpu.make_async_remote_copy(
            src_ref=src, dst_ref=dst, send_sem=ssem, recv_sem=rsem,
            device_id=where, device_id_type=MESH,
        )

    a_copy = remote(a_ref, aoth, a_s, a_r, {"leaf": mate})

    def exchange(i):
        four = pl.ds(4 * chunk(i), 4)
        return remote(xb.at[four, 2], xb.at[four, 1], ex_s.at[i], ex_r.at[i], {"leaf": mate})

    def granule(i, g):
        pull(i, g).wait()
        gi = 2 * chunk(i) + 1 - g
        group = SUBP // 4
        bottom = iota((group, 8, 128), 1) == 7

        def multiply(n):
            at = pl.ds(group * n, group)
            rows = xbuf[i % 2, g, at].reshape(group * GRAN, 256)
            prod = jnp.dot(rows, mc_ref[...], preferred_element_type=f32).reshape(group, 2, 8, 512)
            for q in range(2):
                cols = slice(128 * q, 128 * q + 128)
                nexts = slice(256 + 128 * q, 384 + 128 * q)
                first, second = (pltpu.roll(prod[:, e, :, nexts], 7, 1) for e in range(2))
                u[n, q, 0] = (prod[:, 0, :, cols] + jnp.where(bottom, second, first)).reshape(group * 8, 128)
                third = edge[q, at]
                u[n, q, 1] = (prod[:, 1, :, cols] + jnp.where(bottom, third, second)).reshape(group * 8, 128)
                edge[q, at] = first

        def gather(n):
            for b in range(GRAN):
                half = b % 8 // 4
                plane = 2 * (core if half == 0 else 1 - core)
                tile = 2 * gi + b // 8
                cols = slice(128 * (b % 4), 128 * (b % 4) + 128)
                for q in range(2):
                    own = u[n, q, b // 8, pl.ds(b % 8, group, stride=8), :]
                    xb[tile, plane, SUBP * q + group * n : SUBP * q + group * n + group, cols] = own.astype(bf16)

        for n in range(4):
            multiply(n)
            if n > 0:
                gather(n - 1)
        gather(4 - 1)

    def compress(i):
        @pl.when(i + 1 < NZ)
        def _():
            for g in range(2):
                pull(i + 1, g).start()

        @pl.when((i % 2 == 1) & (i + 1 < NZ))
        def _():
            pull_edge(i + 1).start()

        here = chunk(i)

        @pl.when(i % 2 == 0)
        def _():
            pull_edge(i).wait()
            rows = ebuf[i // 2 % 2].reshape(SUBP * 8, 256)
            prod = jnp.dot(rows, mc_ref[:, 256:512], preferred_element_type=f32).reshape(SUBP, 8, 256)
            for q in range(2):
                edges[(here + 1) % NZ, q] = pltpu.roll(prod[:, :, 128 * q : 128 * q + 128], 7, 1)

        edge[...] = edges[here + 1]

        def both(g, carry):
            granule(i, g)
            return carry

        lax.fori_loop(0, 2, both, 0)
        edges[here] = edge[...]

    rby[:, 12] = jnp.zeros((2, BY, WIDE), bf16)
    rbz[:, 14] = jnp.zeros((2, BZ, WIDE), bf16)
    for d in range(2):
        unsent = slice(COLS, WIDE) if d == 0 else slice(0, COLS)
        rb2[d, 0, :, unsent] = jnp.zeros((BY, COLS), bf16)
        rb3[d, 0, :, unsent] = jnp.zeros((BZ, COLS), bf16)
    edges[NZ] = jnp.zeros((2, SUBP, 8, 128), f32)
    compress(0)
    pl.semaphore_wait(barrier, 4 + NLEAF - 1)
    a_copy.start()
    exchange(0).start()

    a_copy.wait()
    for ref, low, count in ((ay, 0, BY), (az, BY, BZ)):
        for part in range(2):
            rows = slice(128 * part + low, 128 * part + low + count)
            mine, other = a_ref[rows], aoth[rows]
            ref[part * count : (part + 1) * count, 0:128] = mine
            ref[part * count : (part + 1) * count, 128:256] = other
            ref[(2 + part) * count : (3 + part) * count, 0:128] = mine
            ref[(2 + part) * count : (3 + part) * count, 128:256] = -other

    def partial_image(ref, low, count, tile, adds, put):
        par = tile % 2
        beams = slice(low, low + count)
        for at in range(0, COLS, 256):
            cols = slice(at, at + 256)
            imag = slice(COLS + at, COLS + at + 256)
            data = xb[tile, 0:2, :, cols].reshape(256, 256)
            r = jnp.dot(ref[...], data, preferred_element_type=f32)
            c, s = d0_ref[0, par, beams, cols], d0_ref[1, par, beams, cols]
            re = c * r[0:count] - s * r[3 * count :]
            im = c * r[count : 2 * count] + s * r[2 * count : 3 * count]
            for got in adds:
                re = re + got[:, cols].astype(f32)
                im = im + got[:, imag].astype(f32)
            put(cols, re)
            put(imag, im)

    def put_to(ref):
        def put(cols, value):
            ref[:, cols] = value.astype(ref.dtype)
        return put

    def y_to(d):
        return turn_at(z, y + 1 + 2 * d)

    def z_to(d):
        return turn_at(z + 1 + (NZ - 2) * d, y)

    def y_copy(d, k):
        return remote(sby.at[d, k], rby.at[d, k], y_s.at[d, k], y_r.at[d, k], {"turn": y_to(d)})

    def z_copy(d, k):
        return remote(sbz.at[d, k], rbz.at[d, k], z_s.at[d, k], z_r.at[d, k], {"turn": z_to(d)})

    def y_message(c, near, d):
        k = jnp.where(near == 1, 4 + c, c // 2)
        takes = (near == 1) & (c % 2 == d)
        src = jnp.where(takes, c // 2, 12)

        @pl.when(takes)
        def _():
            y_copy(d, c // 2).wait_recv()

        tile = turn_at(chunk(c), y + 2 + near * (2 * d - 1))
        partial_image(ay, 0, BY, tile, (rby.at[d, src],), put_to(sby.at[d, k]))
        y_copy(d, k).start()

    def z_far(d, j):
        tile = turn_at(chunk(0), y + order(j + 2 * d, NY))
        partial_image(az, BY, BZ, tile, (), put_to(sbz.at[d, j]))
        z_copy(d, j).start()

    def z_near(c, j):
        d = (c + 1) % 2
        step = (c - 1) // 2
        k = 2 + 4 * step + j
        takes = (step > 0) | (j // 2 == d)
        prev = jnp.where(step > 0, k - 4, j - 2 * d)
        src = jnp.where(takes, prev, 14)

        @pl.when(takes)
        def _():
            z_copy(d, prev).wait_recv()

        tile = turn_at(chunk(c), y + order(j, NY))
        partial_image(az, BY, BZ, tile, (rbz.at[d, src],), put_to(sbz.at[d, k]))
        z_copy(d, k).start()

    halves = (slice(0, COLS), slice(COLS, WIDE))

    def far2(d):
        part = halves[d]
        return remote(sb2.at[d, 0, :, part], rb2.at[d, 0, :, part], s2_s.at[d, 0], s2_r.at[d, 0], {"turn": z_to(d)})

    def near2(d, k):
        return remote(sb2.at[d, k], rb2.at[d, k], s2_s.at[d, k], s2_r.at[d, k], {"turn": z_to(d)})

    def far3(d):
        part = halves[d]
        return remote(sb3.at[d, 0, :, part], rb3.at[d, 0, :, part], s3_s.at[d, 0], s3_r.at[d, 0], {"turn": y_to(d)})

    def near3(d, k):
        return remote(sb3.at[d, k], rb3.at[d, k], s3_s.at[d, k], s3_r.at[d, k], {"turn": y_to(d)})

    def wait_y(i):
        for d in range(2):
            y_copy(d, 4 + i).wait_recv()
        return (rby.at[0, 4 + i], rby.at[1, 4 + i])

    def wait_z(i):
        for d in range(2):
            z_copy(d, 10 + i).wait_recv()
        return (rbz.at[0, 10 + i], rbz.at[1, 10 + i])

    def put_both(ref):
        def put(cols, value):
            d = 0 if cols.start < COLS else 1
            ref[d, 0, :, cols] = value.astype(bf16)
        return put

    def second_far():
        partial_image(ay, 0, BY, turn_at(z + 4, y), wait_y(0), put_both(sb2))
        for d in range(2):
            far2(d).start()

    def second_y(i):
        d = (i + 1) % 2
        q = (i - 1) // 2
        adds = wait_y(i)
        for side in range(2):
            @pl.when((q == 0) & (d == side))
            def _():
                far2(side).wait_recv()

        @pl.when(q > 0)
        def _():
            near2(d, q).wait_recv()

        partial_image(ay, 0, BY, turn_at(chunk(i), y), adds + (rb2.at[d, q],), put_to(sb2.at[d, q + 1]))
        near2(d, q + 1).start()

    def second_z(i):
        adds = wait_z(i)
        tile = turn_at(z, y + (2, 1, 3, 0)[i])
        if i == 0:
            partial_image(az, BY, BZ, tile, adds, put_both(sb3))
            for d in range(2):
                far3(d).start()
        elif i < 3:
            d = i - 1
            far3(d).wait_recv()
            partial_image(az, BY, BZ, tile, adds + (rb3.at[d, 0],), put_to(sb3.at[d, 1]))
            near3(d, 1).start()
        else:
            for d in range(2):
                near3(d, 1).wait_recv()
            adds = adds + (rb3.at[0, 1], rb3.at[1, 1])
            partial_image(az, BY, BZ, tile, adds, put_to(img.at[pl.ds(BY, BZ)]))

    def main_loop(i, carry):
        @pl.when(i < NZ)
        def _():
            compress(i)
            exchange(i).start()

        @pl.when(i <= NZ)
        def _():
            c = i - 1
            exchange(c).wait_recv()

            def pair(near, carry):
                y_message(c, near, (c + near) % 2)
                return carry

            lax.fori_loop(0, jnp.where(c < 4, 2, 1), pair, 0)

        @pl.when(i == 1)
        def _():
            def far(n, carry):
                z_far(n // 2, n % 2)
                return carry

            lax.fori_loop(0, 4, far, 0)

        @pl.when((i >= 3) & (i <= 8))
        def _():
            def near(j, carry):
                z_near(i - 2, j)
                return carry

            lax.fori_loop(0, 4, near, 0)

        @pl.when((i >= 4) & (i < 12))
        def _():
            def pair(n, carry):
                y_message(i - 4, 1, (i - 4 + n) % 2)
                return carry

            lax.fori_loop(0, jnp.where(i < 8, 1, 2), pair, 0)

        @pl.when(i == 11)
        def _():
            beam = iota((BEAMS, 128), 0)
            odd = 2 * beam + 1 - BEAMS
            bins = iota((BEAMS, 128), 1) + 1 + COLS * core + 2 * COLS * turn
            for level in (1, 2):
                side = (leaf >> level) % 2
                i12[level - 1] = interp(taps_ref[level, side])
                rate = odd * ((2 * side - 1) * (level + 2))
                blocks = phase_blocks(rate * bins + beam * beam * (side + 1), rate * 128, COLS // 128)
                for b, (c, s) in enumerate(blocks):
                    at = slice(128 * b, 128 * b + 128)
                    d12[level - 1, 0, :, at] = c
                    d12[level - 1, 1, :, at] = s

        @pl.when(i == 7)
        def _():
            second_far()

        @pl.when((i > 7) & (i <= 13))
        def _():
            second_y(i - 7)

        @pl.when(i == 10)
        def _():
            second_z(0)

        @pl.when(i == 11)
        def _():
            second_z(1)

        @pl.when(i == 13)
        def _():
            second_z(2)

        return carry

    lax.fori_loop(1, 14, main_loop, 0)
    second_z(3)
    adds = wait_y(7)
    for d in range(2):
        near2(d, 3).wait_recv()
    partial_image(ay, 0, BY, turn, adds + (rb2.at[0, 3], rb2.at[1, 3]), put_to(img.at[pl.ds(0, BY)]))

    for level in range(2):
        value = img[...]
        high = value.astype(bf16)
        low = (value - high.astype(f32)).astype(bf16)
        matrix = i12[level]
        moved = jnp.dot(matrix, high, preferred_element_type=f32) + jnp.dot(matrix, low, preferred_element_type=f32)
        c, s = d12[level, 0], d12[level, 1]
        re = c * moved[:, :COLS] - s * moved[:, COLS:]
        im = c * moved[:, COLS:] + s * moved[:, :COLS]
        target = img if level == 0 else vout
        target[:, :COLS] = re.astype(target.dtype)
        target[:, COLS:] = im.astype(target.dtype)

    def share(e):
        to = (leaf + e) % NLEAF
        rows = pl.ds(pl.multiple_of(16 * to, 16), 16)
        return remote(vout.at[rows], rl.at[leaf], l_s.at[e - 1], l_r.at[e - 1], {"leaf": to})

    def shared(e):
        src = (leaf + NLEAF - e) % NLEAF
        return remote(vout.at[pl.ds(0, 16)], rl.at[src], l_s.at[e - 1], l_r.at[e - 1], {"leaf": mate})

    for e in range(1, NLEAF):
        share(e).start()
    rl[leaf] = vout[pl.ds(pl.multiple_of(16 * leaf, 16), 16)]
    for e in range(1, NLEAF):
        shared(e).wait_recv()
    for side in range(2):
        total = rl[side].astype(f32)
        for xx in range(1, 4):
            total = total + rl[2 * xx + side].astype(f32)
        total = total.astype(bf16)
        for b in range(4):
            out_ref[4 * side + b, :, 0:128] = total[:, 128 * b : 128 * b + 128]
            out_ref[4 * side + b, :, 128:256] = total[:, COLS + 128 * b : COLS + 128 * b + 128]

    def sent_y(k, carry):
        for d in range(2):
            y_copy(d, k).wait_send()
        return carry

    def sent_z(k, carry):
        for d in range(2):
            z_copy(d, k).wait_send()
        return carry

    def sent_mate(i, carry):
        exchange(i).wait_send()
        return carry

    lax.fori_loop(0, NZ, sent_mate, 0)
    lax.fori_loop(0, 12, sent_y, 0)
    lax.fori_loop(0, 14, sent_z, 0)
    for d in range(2):
        far2(d).wait_send()
        far3(d).wait_send()
        near3(d, 1).wait_send()
        for k in range(1, 4):
            near2(d, k).wait_send()
    for e in range(1, NLEAF):
        share(e).wait_send()


def reduce_merge(x, chirp, taps, slots):
    vmem = pl.BlockSpec(memory_space=pltpu.VMEM)
    dma = pltpu.SemaphoreType.DMA
    return pl.pallas_call(
        main_kernel,
        out_shape=jax.ShapeDtypeStruct((8, 16, 256), bf16),
        in_specs=[pl.BlockSpec(memory_space=pl.ANY), vmem, vmem, pl.BlockSpec(memory_space=pltpu.SMEM)],
        out_specs=vmem,
        scratch_shapes=[
            pltpu.VMEM((2, 2, SUBP, GRAN, 256), bf16),
            pltpu.VMEM((2, SUBP, 8, 256), bf16),
            pltpu.VMEM((4, 2, 2, SUBP * 8 // 4, 128), f32),
            pltpu.VMEM((2, SUBP, 8, 128), f32),
            pltpu.VMEM((NZ + 1, 2, SUBP, 8, 128), f32),
            pltpu.VMEM((TILES, 3, 128, COLS), bf16),
            pltpu.VMEM((256, 128), bf16),
            pltpu.VMEM((4 * BY, 256), bf16),
            pltpu.VMEM((4 * BZ, 256), bf16),
            pltpu.VMEM((2, 13, BY, WIDE), bf16),
            pltpu.VMEM((2, 12, BY, WIDE), bf16),
            pltpu.VMEM((2, 15, BZ, WIDE), bf16),
            pltpu.VMEM((2, 14, BZ, WIDE), bf16),
            pltpu.VMEM((2, 4, BY, WIDE), bf16),
            pltpu.VMEM((2, 4, BY, WIDE), bf16),
            pltpu.VMEM((2, 2, BZ, WIDE), bf16),
            pltpu.VMEM((2, 2, BZ, WIDE), bf16),
            pltpu.VMEM((BEAMS, WIDE), f32),
            pltpu.VMEM((BEAMS, WIDE), bf16),
            pltpu.VMEM((NLEAF, 16, WIDE), bf16),
            pltpu.VMEM((2, BEAMS, BEAMS), bf16),
            pltpu.VMEM((2, 2, BEAMS, COLS), f32),
            pltpu.VMEM((256, 512), bf16),
            pltpu.VMEM((256, 128), bf16),
            pltpu.VMEM((2, 2, BEAMS, COLS), f32),
            dma((2, 2)), dma((2,)), dma((NZ,)), dma((NZ,)), dma, dma,
            dma((2, 12)), dma((2, 12)), dma((2, 14)), dma((2, 14)),
            dma((2, 4)), dma((2, 4)), dma((2, 2)), dma((2, 2)),
            dma((NLEAF - 1,)), dma((NLEAF - 1,)),
        ],
        compiler_params=pltpu.CompilerParams(
            collective_id=0, has_side_effects=True, vmem_limit_bytes=60 * 1024 * 1024
        ),
        name="reduce_merge",
    )(x, chirp, taps, slots)


def per_device(echoes, chirp, taps, slots):
    taps = jnp.transpose(taps, (0, 1, 3, 2))
    image = reduce_merge(echoes, chirp, taps, slots)
    return jnp.transpose(image, (1, 0, 2))


def solution(mesh):
    placed = (P(("leaf", "turn"), None, None), P(), P(), P("leaf", None))
    return jax.shard_map(
        per_device, mesh=mesh, in_specs=placed, out_specs=P("leaf", "turn", None), check_vma=False
    )
```

```python
import functools
import math

import jax
import jax.numpy as jnp
from jax import lax
from jax.experimental import pallas as pl
from jax.experimental.pallas import tpu as pltpu
from jax.sharding import PartitionSpec as P

WEIGHTS = (-1.0 / 32, 3.0 / 32, -7.0 / 32, 21.0 / 32, 21.0 / 32, -7.0 / 32, 3.0 / 32, -1.0 / 32)
MESH = pl.DeviceIdType.MESH

BEAMS = 128
TAPS = 8
SUBP = 64
NSUB = 32
NZ = 8
NY = 4
NLEAF = 8
TILES = NZ * NY
COLS = 512
WIDE = 2 * COLS
BY = 80
BZ = BEAMS - BY
GRAN = 16
NGRAN = 256 // GRAN

f32 = jnp.float32
bf16 = jnp.bfloat16


def cos_sin(n):
    n = n & 4095
    quad = (n + 512) >> 10
    m = (n - (quad << 10)).astype(f32) * (2.0 * math.pi / 4096)
    m2 = m * m
    s = m * (1.0 + m2 * (-1.0 / 6 + m2 * (1.0 / 120 + m2 * (-1.0 / 5040 + m2 * (1.0 / 362880)))))
    c = 1.0 + m2 * (-0.5 + m2 * (1.0 / 24 + m2 * (-1.0 / 720 + m2 * (1.0 / 40320))))
    odd = (quad & 1) == 1
    cc = jnp.where(odd, s, c)
    ss = jnp.where(odd, c, s)
    cos = jnp.where((quad == 1) | (quad == 2), -cc, cc)
    sin = jnp.where((quad == 2) | (quad == 3), -ss, ss)
    return cos, sin


def iota(shape, dim):
    return lax.broadcasted_iota(jnp.int32, shape, dim)


def interp(rows):
    cells = iota((BEAMS, BEAMS), 0)
    total = jnp.zeros((BEAMS, BEAMS), f32)
    for t in range(TAPS):
        total = total + jnp.where(rows[t : t + 1, :] == cells, WEIGHTS[t], 0.0)
    return total.T.astype(bf16)


def phase_blocks(first, step, count):
    c, s = cos_sin(first)
    blocks = [(c, s)]
    fc, fs = cos_sin(step)
    for _ in range(count - 1):
        c, s = c * fc - s * fs, s * fc + c * fs
        blocks.append((c, s))
    return blocks


def first_tables(chirp_ref, taps_ref, slots_ref, mc_ref, a_ref, d0_ref):
    leaf = lax.axis_index("leaf")
    turn = lax.axis_index("turn")
    core = leaf % 2
    sq = (BEAMS, BEAMS)

    g = jnp.broadcast_to(chirp_ref[...][:, None, :], (2, 8, 128)).reshape(16, 128)
    flip = ((iota(sq, 0) + iota(sq, 1)) % 128 == 0).astype(bf16)
    h = jnp.dot(g, flip, preferred_element_type=f32)
    lower = iota(sq, 0) >= iota(sq, 1)
    tabs = []
    for part in range(2):
        row = jnp.broadcast_to(h[8 * part : 8 * part + 1], sq)
        tabs.append(pltpu.roll(row, 0, 1, stride=1, stride_axis=0))
    for side in range(2):
        re, im = (jnp.where(lower if side == 0 else ~lower, t, 0.0) for t in tabs)
        at = 256 * side
        mc_ref[0:128, at : at + 128] = re.astype(bf16)
        mc_ref[0:128, at + 128 : at + 256] = im.astype(bf16)
        mc_ref[128:256, at : at + 128] = (-im).astype(bf16)
        mc_ref[128:256, at + 128 : at + 256] = re.astype(bf16)

    slot = slots_ref[0, turn]
    beam = iota(sq, 0)
    lane = iota(sq, 1)
    m = lane % SUBP
    n = (2 * beam + 1 - BEAMS) * (2 * m + 1 - SUBP) + 3 * (beam + 1) * (2 * slot + 1) * (2 * m + 1)
    cos, sin = cos_sin(8 * n)
    scale = 1.0 / math.sqrt(2.0 * NSUB * SUBP)
    cos, sin = cos * scale, sin * scale
    first = lane < SUBP
    s_re = jnp.where(first, cos, -sin).astype(bf16)
    s_im = jnp.where(first, sin, cos).astype(bf16)
    i0 = interp(taps_ref[0, core])
    z_re = jnp.dot(i0, s_re, preferred_element_type=f32)
    z_im = jnp.dot(i0, s_im, preferred_element_type=f32)
    ca, sa = cos_sin(beam * beam * (core + 1))
    a_ref[0:128] = (ca * z_re - sa * z_im).astype(bf16)
    a_ref[128:256] = (ca * z_im + sa * z_re).astype(bf16)

    odd = 2 * beam + 1 - BEAMS
    sign = (2 * core - 1).astype(f32)
    blocks = phase_blocks(2 * odd * (lane + COLS * core + 1), 2 * odd * 128, COLS // 128)
    for b, (c, s) in enumerate(blocks):
        at = slice(128 * b, 128 * b + 128)
        d0_ref[0, 0, :, at] = c
        d0_ref[0, 1, :, at] = -c
        d0_ref[1, 0, :, at] = s * sign
        d0_ref[1, 1, :, at] = -s * sign


def main_kernel(
    x_ref, chirp_ref, taps_ref, slots_ref, out_ref,
    xbuf, ebuf, u, edge, edges, xb, aoth, ay, az,
    rby, sby, rbz, sbz, rb2, sb2, rb3, sb3, img, vout, rl, i12, d12, mc_ref, a_ref, d0_ref,
    in_sem, e_sem, ex_s, ex_r, a_s, a_r, y_s, y_r, z_s, z_r, s2_s, s2_r, s3_s, s3_r, l_s, l_r,
):
    leaf = lax.axis_index("leaf")
    turn = lax.axis_index("turn")
    core = leaf % 2
    z = turn // NY
    y = turn % NY
    mate = leaf + 1 - 2 * core

    def turn_at(zz, yy):
        return (zz % NZ) * NY + yy % NY

    ynbr = (turn_at(z, y + 1), turn_at(z, y + NY - 1))
    znbr = (turn_at(z + 1, y), turn_at(z + NZ - 1, y))

    def order(i, n):
        step = (i + 1) // 2
        return n // 2 + (1 - 2 * (i % 2)) * step

    def chunk(i):
        return (z + order(i, NZ)) % NZ

    def pull(i, g):
        at = pl.multiple_of((2 * chunk(i) + 1 - g) * GRAN, GRAN)
        return pltpu.make_async_copy(x_ref.at[:, pl.ds(at, GRAN), :], xbuf.at[i % 2, g], in_sem.at[i % 2, g])

    def pull_edge(i):
        at = pl.multiple_of((chunk(i) + 1) % NZ * 2 * GRAN, 8)
        slot = i // 2 % 2
        return pltpu.make_async_copy(x_ref.at[:, pl.ds(at, 8), :], ebuf.at[slot], e_sem.at[slot])

    pull_edge(0).start()
    for g in range(2):
        pull(0, g).start()

    barrier = pltpu.get_barrier_semaphore()
    for t in ynbr + znbr:
        pl.semaphore_signal(barrier, inc=1, device_id={"turn": t}, device_id_type=MESH)
    for e in range(1, NLEAF):
        pl.semaphore_signal(barrier, inc=1, device_id={"leaf": (leaf + e) % NLEAF}, device_id_type=MESH)
    first_tables(chirp_ref, taps_ref, slots_ref, mc_ref, a_ref, d0_ref)

    def remote(src, dst, ssem, rsem, where):
        return pltpu.make_async_remote_copy(
            src_ref=src, dst_ref=dst, send_sem=ssem, recv_sem=rsem,
            device_id=where, device_id_type=MESH,
        )

    a_copy = remote(a_ref, aoth, a_s, a_r, {"leaf": mate})

    def exchange(i):
        four = pl.ds(4 * chunk(i), 4)
        return remote(xb.at[four, 2], xb.at[four, 1], ex_s.at[i], ex_r.at[i], {"leaf": mate})

    def granule(i, g):
        pull(i, g).wait()
        gi = 2 * chunk(i) + 1 - g
        group = SUBP // 4
        bottom = iota((group, 8, 128), 1) == 7

        def multiply(n):
            at = pl.ds(group * n, group)
            rows = xbuf[i % 2, g, at].reshape(group * GRAN, 256)
            prod = jnp.dot(rows, mc_ref[...], preferred_element_type=f32).reshape(group, 2, 8, 512)
            for q in range(2):
                cols = slice(128 * q, 128 * q + 128)
                nexts = slice(256 + 128 * q, 384 + 128 * q)
                first, second = (pltpu.roll(prod[:, e, :, nexts], 7, 1) for e in range(2))
                u[n, q, 0] = (prod[:, 0, :, cols] + jnp.where(bottom, second, first)).reshape(group * 8, 128)
                third = edge[q, at]
                u[n, q, 1] = (prod[:, 1, :, cols] + jnp.where(bottom, third, second)).reshape(group * 8, 128)
                edge[q, at] = first

        def gather(n):
            for b in range(GRAN):
                half = b % 8 // 4
                plane = 2 * (core if half == 0 else 1 - core)
                tile = 2 * gi + b // 8
                cols = slice(128 * (b % 4), 128 * (b % 4) + 128)
                for q in range(2):
                    own = u[n, q, b // 8, pl.ds(b % 8, group, stride=8), :]
                    xb[tile, plane, SUBP * q + group * n : SUBP * q + group * n + group, cols] = own.astype(bf16)

        for n in range(4):
            multiply(n)
            if n > 0:
                gather(n - 1)
        gather(4 - 1)

    def compress(i):
        @pl.when(i + 1 < NZ)
        def _():
            for g in range(2):
                pull(i + 1, g).start()

        @pl.when((i % 2 == 1) & (i + 1 < NZ))
        def _():
            pull_edge(i + 1).start()

        here = chunk(i)

        @pl.when(i % 2 == 0)
        def _():
            pull_edge(i).wait()
            rows = ebuf[i // 2 % 2].reshape(SUBP * 8, 256)
            prod = jnp.dot(rows, mc_ref[:, 256:512], preferred_element_type=f32).reshape(SUBP, 8, 256)
            for q in range(2):
                edges[(here + 1) % NZ, q] = pltpu.roll(prod[:, :, 128 * q : 128 * q + 128], 7, 1)

        edge[...] = edges[here + 1]

        def both(g, carry):
            granule(i, g)
            return carry

        lax.fori_loop(0, 2, both, 0)
        edges[here] = edge[...]

    rby[:, 12] = jnp.zeros((2, BY, WIDE), bf16)
    rbz[:, 14] = jnp.zeros((2, BZ, WIDE), bf16)
    for d in range(2):
        unsent = slice(COLS, WIDE) if d == 0 else slice(0, COLS)
        rb2[d, 0, :, unsent] = jnp.zeros((BY, COLS), bf16)
        rb3[d, 0, :, unsent] = jnp.zeros((BZ, COLS), bf16)
    edges[NZ] = jnp.zeros((2, SUBP, 8, 128), f32)
    compress(0)
    pl.semaphore_wait(barrier, 4 + NLEAF - 1)
    a_copy.start()
    exchange(0).start()

    a_copy.wait()
    for ref, low, count in ((ay, 0, BY), (az, BY, BZ)):
        for part in range(2):
            rows = slice(128 * part + low, 128 * part + low + count)
            mine, other = a_ref[rows], aoth[rows]
            ref[part * count : (part + 1) * count, 0:128] = mine
            ref[part * count : (part + 1) * count, 128:256] = other
            ref[(2 + part) * count : (3 + part) * count, 0:128] = mine
            ref[(2 + part) * count : (3 + part) * count, 128:256] = -other

    def partial_image(ref, low, count, tile, adds, put):
        par = tile % 2
        beams = slice(low, low + count)
        for at in range(0, COLS, 256):
            cols = slice(at, at + 256)
            imag = slice(COLS + at, COLS + at + 256)
            data = xb[tile, 0:2, :, cols].reshape(256, 256)
            r = jnp.dot(ref[...], data, preferred_element_type=f32)
            c, s = d0_ref[0, par, beams, cols], d0_ref[1, par, beams, cols]
            re = c * r[0:count] - s * r[3 * count :]
            im = c * r[count : 2 * count] + s * r[2 * count : 3 * count]
            for got in adds:
                re = re + got[:, cols].astype(f32)
                im = im + got[:, imag].astype(f32)
            put(cols, re)
            put(imag, im)

    def put_to(ref):
        def put(cols, value):
            ref[:, cols] = value.astype(ref.dtype)
        return put

    def y_to(d):
        return turn_at(z, y + 1 + 2 * d)

    def z_to(d):
        return turn_at(z + 1 + (NZ - 2) * d, y)

    def y_copy(d, k):
        return remote(sby.at[d, k], rby.at[d, k], y_s.at[d, k], y_r.at[d, k], {"turn": y_to(d)})

    def z_copy(d, k):
        return remote(sbz.at[d, k], rbz.at[d, k], z_s.at[d, k], z_r.at[d, k], {"turn": z_to(d)})

    def y_message(c, near, d):
        k = jnp.where(near == 1, 4 + c, c // 2)
        takes = (near == 1) & (c % 2 == d)
        src = jnp.where(takes, c // 2, 12)

        @pl.when(takes)
        def _():
            y_copy(d, c // 2).wait_recv()

        tile = turn_at(chunk(c), y + 2 + near * (2 * d - 1))
        partial_image(ay, 0, BY, tile, (rby.at[d, src],), put_to(sby.at[d, k]))
        y_copy(d, k).start()

    def z_far(d, j):
        tile = turn_at(chunk(0), y + order(j + 2 * d, NY))
        partial_image(az, BY, BZ, tile, (), put_to(sbz.at[d, j]))
        z_copy(d, j).start()

    def z_near(c, j):
        d = (c + 1) % 2
        step = (c - 1) // 2
        k = 2 + 4 * step + j
        takes = (step > 0) | (j // 2 == d)
        prev = jnp.where(step > 0, k - 4, j - 2 * d)
        src = jnp.where(takes, prev, 14)

        @pl.when(takes)
        def _():
            z_copy(d, prev).wait_recv()

        tile = turn_at(chunk(c), y + order(j, NY))
        partial_image(az, BY, BZ, tile, (rbz.at[d, src],), put_to(sbz.at[d, k]))
        z_copy(d, k).start()

    halves = (slice(0, COLS), slice(COLS, WIDE))

    def far2(d):
        part = halves[d]
        return remote(sb2.at[d, 0, :, part], rb2.at[d, 0, :, part], s2_s.at[d, 0], s2_r.at[d, 0], {"turn": z_to(d)})

    def near2(d, k):
        return remote(sb2.at[d, k], rb2.at[d, k], s2_s.at[d, k], s2_r.at[d, k], {"turn": z_to(d)})

    def far3(d):
        part = halves[d]
        return remote(sb3.at[d, 0, :, part], rb3.at[d, 0, :, part], s3_s.at[d, 0], s3_r.at[d, 0], {"turn": y_to(d)})

    def near3(d, k):
        return remote(sb3.at[d, k], rb3.at[d, k], s3_s.at[d, k], s3_r.at[d, k], {"turn": y_to(d)})

    def wait_y(i):
        for d in range(2):
            y_copy(d, 4 + i).wait_recv()
        return (rby.at[0, 4 + i], rby.at[1, 4 + i])

    def wait_z(i):
        for d in range(2):
            z_copy(d, 10 + i).wait_recv()
        return (rbz.at[0, 10 + i], rbz.at[1, 10 + i])

    def put_both(ref):
        def put(cols, value):
            d = 0 if cols.start < COLS else 1
            ref[d, 0, :, cols] = value.astype(bf16)
        return put

    def second_far():
        partial_image(ay, 0, BY, turn_at(z + 4, y), wait_y(0), put_both(sb2))
        for d in range(2):
            far2(d).start()

    def second_y(i):
        d = (i + 1) % 2
        q = (i - 1) // 2
        adds = wait_y(i)
        for side in range(2):
            @pl.when((q == 0) & (d == side))
            def _():
                far2(side).wait_recv()

        @pl.when(q > 0)
        def _():
            near2(d, q).wait_recv()

        partial_image(ay, 0, BY, turn_at(chunk(i), y), adds + (rb2.at[d, q],), put_to(sb2.at[d, q + 1]))
        near2(d, q + 1).start()

    def second_z(i):
        adds = wait_z(i)
        tile = turn_at(z, y + (2, 1, 3, 0)[i])
        if i == 0:
            partial_image(az, BY, BZ, tile, adds, put_both(sb3))
            for d in range(2):
                far3(d).start()
        elif i < 3:
            d = i - 1
            far3(d).wait_recv()
            partial_image(az, BY, BZ, tile, adds + (rb3.at[d, 0],), put_to(sb3.at[d, 1]))
            near3(d, 1).start()
        else:
            for d in range(2):
                near3(d, 1).wait_recv()
            adds = adds + (rb3.at[0, 1], rb3.at[1, 1])
            partial_image(az, BY, BZ, tile, adds, put_to(img.at[pl.ds(BY, BZ)]))

    def main_loop(i, carry):
        @pl.when(i < NZ)
        def _():
            compress(i)
            exchange(i).start()

        @pl.when(i <= NZ)
        def _():
            c = i - 1
            exchange(c).wait_recv()

            def pair(near, carry):
                y_message(c, near, (c + near) % 2)
                return carry

            lax.fori_loop(0, jnp.where(c < 2, 2, 1), pair, 0)

        @pl.when(i == 1)
        def _():
            def far(n, carry):
                z_far(n // 2, n % 2)
                return carry

            lax.fori_loop(0, 4, far, 0)

        @pl.when((i >= 4) & (i <= 9))
        def _():
            def near(j, carry):
                z_near(i - 3, j)
                return carry

            lax.fori_loop(0, 4, near, 0)

        @pl.when((i >= 4) & (i < 12))
        def _():
            def pair(n, carry):
                y_message(i - 4, 1, (i - 4 + n) % 2)
                return carry

            lax.fori_loop(0, jnp.where(i < 6, 1, 2), pair, 0)

        @pl.when(i == 11)
        def _():
            beam = iota((BEAMS, 128), 0)
            odd = 2 * beam + 1 - BEAMS
            bins = iota((BEAMS, 128), 1) + 1 + COLS * core + 2 * COLS * turn
            for level in (1, 2):
                side = (leaf >> level) % 2
                i12[level - 1] = interp(taps_ref[level, side])
                rate = odd * ((2 * side - 1) * (level + 2))
                blocks = phase_blocks(rate * bins + beam * beam * (side + 1), rate * 128, COLS // 128)
                for b, (c, s) in enumerate(blocks):
                    at = slice(128 * b, 128 * b + 128)
                    d12[level - 1, 0, :, at] = c
                    d12[level - 1, 1, :, at] = s

        @pl.when(i == 6)
        def _():
            second_far()

        @pl.when((i > 6) & (i <= 12))
        def _():
            second_y(i - 6)

        @pl.when(i == 10)
        def _():
            second_z(0)

        @pl.when(i == 11)
        def _():
            second_z(1)

        @pl.when(i == 13)
        def _():
            second_z(2)

        return carry

    lax.fori_loop(1, 14, main_loop, 0)
    second_z(3)
    adds = wait_y(7)
    for d in range(2):
        near2(d, 3).wait_recv()
    partial_image(ay, 0, BY, turn, adds + (rb2.at[0, 3], rb2.at[1, 3]), put_to(img.at[pl.ds(0, BY)]))

    for level in range(2):
        value = img[...]
        high = value.astype(bf16)
        low = (value - high.astype(f32)).astype(bf16)
        matrix = i12[level]
        moved = jnp.dot(matrix, high, preferred_element_type=f32) + jnp.dot(matrix, low, preferred_element_type=f32)
        c, s = d12[level, 0], d12[level, 1]
        re = c * moved[:, :COLS] - s * moved[:, COLS:]
        im = c * moved[:, COLS:] + s * moved[:, :COLS]
        target = img if level == 0 else vout
        target[:, :COLS] = re.astype(target.dtype)
        target[:, COLS:] = im.astype(target.dtype)

    def share(e):
        to = (leaf + e) % NLEAF
        rows = pl.ds(pl.multiple_of(16 * to, 16), 16)
        return remote(vout.at[rows], rl.at[leaf], l_s.at[e - 1], l_r.at[e - 1], {"leaf": to})

    def shared(e):
        src = (leaf + NLEAF - e) % NLEAF
        return remote(vout.at[pl.ds(0, 16)], rl.at[src], l_s.at[e - 1], l_r.at[e - 1], {"leaf": mate})

    for e in range(1, NLEAF):
        share(e).start()
    rl[leaf] = vout[pl.ds(pl.multiple_of(16 * leaf, 16), 16)]
    def sent_y(k, carry):
        for d in range(2):
            y_copy(d, k).wait_send()
        return carry

    def sent_z(k, carry):
        for d in range(2):
            z_copy(d, k).wait_send()
        return carry

    def sent_mate(i, carry):
        exchange(i).wait_send()
        return carry

    lax.fori_loop(0, NZ, sent_mate, 0)
    lax.fori_loop(0, 12, sent_y, 0)
    lax.fori_loop(0, 14, sent_z, 0)
    for d in range(2):
        far2(d).wait_send()
        far3(d).wait_send()
        near3(d, 1).wait_send()
        for k in range(1, 4):
            near2(d, k).wait_send()

    for e in range(1, NLEAF):
        shared(e).wait_recv()
    for side in range(2):
        total = rl[side].astype(f32)
        for xx in range(1, 4):
            total = total + rl[2 * xx + side].astype(f32)
        total = total.astype(bf16)
        for b in range(4):
            out_ref[4 * side + b, :, 0:128] = total[:, 128 * b : 128 * b + 128]
            out_ref[4 * side + b, :, 128:256] = total[:, COLS + 128 * b : COLS + 128 * b + 128]

    for e in range(1, NLEAF):
        share(e).wait_send()


def reduce_merge(x, chirp, taps, slots):
    vmem = pl.BlockSpec(memory_space=pltpu.VMEM)
    dma = pltpu.SemaphoreType.DMA
    return pl.pallas_call(
        main_kernel,
        out_shape=jax.ShapeDtypeStruct((8, 16, 256), bf16),
        in_specs=[pl.BlockSpec(memory_space=pl.ANY), vmem, vmem, pl.BlockSpec(memory_space=pltpu.SMEM)],
        out_specs=vmem,
        scratch_shapes=[
            pltpu.VMEM((2, 2, SUBP, GRAN, 256), bf16),
            pltpu.VMEM((2, SUBP, 8, 256), bf16),
            pltpu.VMEM((4, 2, 2, SUBP * 8 // 4, 128), f32),
            pltpu.VMEM((2, SUBP, 8, 128), f32),
            pltpu.VMEM((NZ + 1, 2, SUBP, 8, 128), f32),
            pltpu.VMEM((TILES, 3, 128, COLS), bf16),
            pltpu.VMEM((256, 128), bf16),
            pltpu.VMEM((4 * BY, 256), bf16),
            pltpu.VMEM((4 * BZ, 256), bf16),
            pltpu.VMEM((2, 13, BY, WIDE), bf16),
            pltpu.VMEM((2, 12, BY, WIDE), bf16),
            pltpu.VMEM((2, 15, BZ, WIDE), bf16),
            pltpu.VMEM((2, 14, BZ, WIDE), bf16),
            pltpu.VMEM((2, 4, BY, WIDE), bf16),
            pltpu.VMEM((2, 4, BY, WIDE), bf16),
            pltpu.VMEM((2, 2, BZ, WIDE), bf16),
            pltpu.VMEM((2, 2, BZ, WIDE), bf16),
            pltpu.VMEM((BEAMS, WIDE), f32),
            pltpu.VMEM((BEAMS, WIDE), bf16),
            pltpu.VMEM((NLEAF, 16, WIDE), bf16),
            pltpu.VMEM((2, BEAMS, BEAMS), bf16),
            pltpu.VMEM((2, 2, BEAMS, COLS), f32),
            pltpu.VMEM((256, 512), bf16),
            pltpu.VMEM((256, 128), bf16),
            pltpu.VMEM((2, 2, BEAMS, COLS), f32),
            dma((2, 2)), dma((2,)), dma((NZ,)), dma((NZ,)), dma, dma,
            dma((2, 12)), dma((2, 12)), dma((2, 14)), dma((2, 14)),
            dma((2, 4)), dma((2, 4)), dma((2, 2)), dma((2, 2)),
            dma((NLEAF - 1,)), dma((NLEAF - 1,)),
        ],
        compiler_params=pltpu.CompilerParams(
            collective_id=0, has_side_effects=True, vmem_limit_bytes=60 * 1024 * 1024
        ),
        name="reduce_merge",
    )(x, chirp, taps, slots)


def per_device(echoes, chirp, taps, slots):
    taps = jnp.transpose(taps, (0, 1, 3, 2))
    image = reduce_merge(echoes, chirp, taps, slots)
    return jnp.transpose(image, (1, 0, 2))


def solution(mesh):
    placed = (P(("leaf", "turn"), None, None), P(), P(), P("leaf", None))
    return jax.shard_map(
        per_device, mesh=mesh, in_specs=placed, out_specs=P("leaf", "turn", None), check_vma=False
    )
```

```python
import functools
import math

import jax
import jax.numpy as jnp
from jax import lax
from jax.experimental import pallas as pl
from jax.experimental.pallas import tpu as pltpu
from jax.sharding import PartitionSpec as P

WEIGHTS = (-1.0 / 32, 3.0 / 32, -7.0 / 32, 21.0 / 32, 21.0 / 32, -7.0 / 32, 3.0 / 32, -1.0 / 32)
MESH = pl.DeviceIdType.MESH

BEAMS = 128
TAPS = 8
SUBP = 64
NSUB = 32
NZ = 8
NY = 4
NLEAF = 8
TILES = NZ * NY
COLS = 512
WIDE = 2 * COLS
BY = 80
BZ = BEAMS - BY
GRAN = 16
NGRAN = 256 // GRAN

f32 = jnp.float32
bf16 = jnp.bfloat16


def cos_sin(n):
    n = n & 4095
    quad = (n + 512) >> 10
    m = (n - (quad << 10)).astype(f32) * (2.0 * math.pi / 4096)
    m2 = m * m
    s = m * (1.0 + m2 * (-1.0 / 6 + m2 * (1.0 / 120 + m2 * (-1.0 / 5040 + m2 * (1.0 / 362880)))))
    c = 1.0 + m2 * (-0.5 + m2 * (1.0 / 24 + m2 * (-1.0 / 720 + m2 * (1.0 / 40320))))
    odd = (quad & 1) == 1
    cc = jnp.where(odd, s, c)
    ss = jnp.where(odd, c, s)
    cos = jnp.where((quad == 1) | (quad == 2), -cc, cc)
    sin = jnp.where((quad == 2) | (quad == 3), -ss, ss)
    return cos, sin


def iota(shape, dim):
    return lax.broadcasted_iota(jnp.int32, shape, dim)


def interp(rows):
    cells = iota((BEAMS, BEAMS), 0)
    total = jnp.zeros((BEAMS, BEAMS), f32)
    for t in range(TAPS):
        total = total + jnp.where(rows[t : t + 1, :] == cells, WEIGHTS[t], 0.0)
    return total.T.astype(bf16)


def phase_blocks(first, step, count):
    c, s = cos_sin(first)
    blocks = [(c, s)]
    fc, fs = cos_sin(step)
    for _ in range(count - 1):
        c, s = c * fc - s * fs, s * fc + c * fs
        blocks.append((c, s))
    return blocks


def first_tables(chirp_ref, taps_ref, slots_ref, mc_ref, a_ref, d0_ref):
    leaf = lax.axis_index("leaf")
    turn = lax.axis_index("turn")
    core = leaf % 2
    sq = (BEAMS, BEAMS)

    g = jnp.broadcast_to(chirp_ref[...][:, None, :], (2, 8, 128)).reshape(16, 128)
    flip = ((iota(sq, 0) + iota(sq, 1)) % 128 == 0).astype(bf16)
    h = jnp.dot(g, flip, preferred_element_type=f32)
    lower = iota(sq, 0) >= iota(sq, 1)
    tabs = []
    for part in range(2):
        row = jnp.broadcast_to(h[8 * part : 8 * part + 1], sq)
        tabs.append(pltpu.roll(row, 0, 1, stride=1, stride_axis=0))
    for side in range(2):
        re, im = (jnp.where(lower if side == 0 else ~lower, t, 0.0) for t in tabs)
        at = 256 * side
        mc_ref[0:128, at : at + 128] = re.astype(bf16)
        mc_ref[0:128, at + 128 : at + 256] = im.astype(bf16)
        mc_ref[128:256, at : at + 128] = (-im).astype(bf16)
        mc_ref[128:256, at + 128 : at + 256] = re.astype(bf16)

    slot = slots_ref[0, turn]
    beam = iota(sq, 0)
    lane = iota(sq, 1)
    m = lane % SUBP
    n = (2 * beam + 1 - BEAMS) * (2 * m + 1 - SUBP) + 3 * (beam + 1) * (2 * slot + 1) * (2 * m + 1)
    cos, sin = cos_sin(8 * n)
    scale = 1.0 / math.sqrt(2.0 * NSUB * SUBP)
    cos, sin = cos * scale, sin * scale
    first = lane < SUBP
    s_re = jnp.where(first, cos, -sin).astype(bf16)
    s_im = jnp.where(first, sin, cos).astype(bf16)
    i0 = interp(taps_ref[0, core])
    z_re = jnp.dot(i0, s_re, preferred_element_type=f32)
    z_im = jnp.dot(i0, s_im, preferred_element_type=f32)
    ca, sa = cos_sin(beam * beam * (core + 1))
    a_ref[0:128] = (ca * z_re - sa * z_im).astype(bf16)
    a_ref[128:256] = (ca * z_im + sa * z_re).astype(bf16)

    odd = 2 * beam + 1 - BEAMS
    sign = (2 * core - 1).astype(f32)
    blocks = phase_blocks(2 * odd * (lane + COLS * core + 1), 2 * odd * 128, COLS // 128)
    for b, (c, s) in enumerate(blocks):
        at = slice(128 * b, 128 * b + 128)
        d0_ref[0, 0, :, at] = c
        d0_ref[0, 1, :, at] = -c
        d0_ref[1, 0, :, at] = s * sign
        d0_ref[1, 1, :, at] = -s * sign


def main_kernel(
    x_ref, chirp_ref, taps_ref, slots_ref, out_ref,
    xbuf, ebuf, u, edge, edges, xb, aoth, ay, az,
    rby, sby, rbz, sbz, rb2, sb2, rb3, sb3, img, vout, rl, i12, d12, mc_ref, a_ref, d0_ref,
    in_sem, e_sem, ex_s, ex_r, a_s, a_r, y_s, y_r, z_s, z_r, s2_s, s2_r, s3_s, s3_r, l_s, l_r,
):
    leaf = lax.axis_index("leaf")
    turn = lax.axis_index("turn")
    core = leaf % 2
    z = turn // NY
    y = turn % NY
    mate = leaf + 1 - 2 * core

    def turn_at(zz, yy):
        return (zz % NZ) * NY + yy % NY

    ynbr = (turn_at(z, y + 1), turn_at(z, y + NY - 1))
    znbr = (turn_at(z + 1, y), turn_at(z + NZ - 1, y))

    def order(i, n):
        step = (i + 1) // 2
        return n // 2 + (1 - 2 * (i % 2)) * step

    def chunk(i):
        return (z + order(i, NZ)) % NZ

    def pull(i, g):
        at = pl.multiple_of((2 * chunk(i) + 1 - g) * GRAN, GRAN)
        return pltpu.make_async_copy(x_ref.at[:, pl.ds(at, GRAN), :], xbuf.at[i % 2, g], in_sem.at[i % 2, g])

    def pull_edge(i):
        at = pl.multiple_of((chunk(i) + 1) % NZ * 2 * GRAN, 8)
        slot = i // 2 % 2
        return pltpu.make_async_copy(x_ref.at[:, pl.ds(at, 8), :], ebuf.at[slot], e_sem.at[slot])

    pull_edge(0).start()
    for g in range(2):
        pull(0, g).start()

    barrier = pltpu.get_barrier_semaphore()
    for t in ynbr + znbr:
        pl.semaphore_signal(barrier, inc=1, device_id={"turn": t}, device_id_type=MESH)
    for e in range(1, NLEAF):
        pl.semaphore_signal(barrier, inc=1, device_id={"leaf": (leaf + e) % NLEAF}, device_id_type=MESH)
    first_tables(chirp_ref, taps_ref, slots_ref, mc_ref, a_ref, d0_ref)

    def remote(src, dst, ssem, rsem, where):
        return pltpu.make_async_remote_copy(
            src_ref=src, dst_ref=dst, send_sem=ssem, recv_sem=rsem,
            device_id=where, device_id_type=MESH,
        )

    a_copy = remote(a_ref, aoth, a_s, a_r, {"leaf": mate})

    def exchange(i):
        four = pl.ds(4 * chunk(i), 4)
        return remote(xb.at[four, 2], xb.at[four, 1], ex_s.at[i], ex_r.at[i], {"leaf": mate})

    def granule(i, g):
        pull(i, g).wait()
        gi = 2 * chunk(i) + 1 - g
        group = SUBP // 4
        bottom = iota((group, 8, 128), 1) == 7

        def multiply(n):
            at = pl.ds(group * n, group)
            rows = xbuf[i % 2, g, at].reshape(group * GRAN, 256)
            prod = jnp.dot(rows, mc_ref[...], preferred_element_type=f32).reshape(group, 2, 8, 512)
            for q in range(2):
                cols = slice(128 * q, 128 * q + 128)
                nexts = slice(256 + 128 * q, 384 + 128 * q)
                first, second = (pltpu.roll(prod[:, e, :, nexts], 7, 1) for e in range(2))
                u[n, q, 0] = (prod[:, 0, :, cols] + jnp.where(bottom, second, first)).reshape(group * 8, 128)
                third = edge[q, at]
                u[n, q, 1] = (prod[:, 1, :, cols] + jnp.where(bottom, third, second)).reshape(group * 8, 128)
                edge[q, at] = first

        def gather(n):
            for b in range(GRAN):
                half = b % 8 // 4
                plane = 2 * (core if half == 0 else 1 - core)
                tile = 2 * gi + b // 8
                cols = slice(128 * (b % 4), 128 * (b % 4) + 128)
                for q in range(2):
                    own = u[n, q, b // 8, pl.ds(b % 8, group, stride=8), :]
                    xb[tile, plane, SUBP * q + group * n : SUBP * q + group * n + group, cols] = own.astype(bf16)

        for n in range(4):
            multiply(n)
            if n > 0:
                gather(n - 1)
        gather(4 - 1)

    def compress(i):
        @pl.when(i + 1 < NZ)
        def _():
            for g in range(2):
                pull(i + 1, g).start()

        @pl.when((i % 2 == 1) & (i + 1 < NZ))
        def _():
            pull_edge(i + 1).start()

        here = chunk(i)

        @pl.when(i % 2 == 0)
        def _():
            pull_edge(i).wait()
            rows = ebuf[i // 2 % 2].reshape(SUBP * 8, 256)
            prod = jnp.dot(rows, mc_ref[:, 256:512], preferred_element_type=f32).reshape(SUBP, 8, 256)
            for q in range(2):
                edges[(here + 1) % NZ, q] = pltpu.roll(prod[:, :, 128 * q : 128 * q + 128], 7, 1)

        edge[...] = edges[here + 1]

        def both(g, carry):
            granule(i, g)
            return carry

        lax.fori_loop(0, 2, both, 0)
        edges[here] = edge[...]

    rby[:, 12] = jnp.zeros((2, BY, WIDE), bf16)
    rbz[:, 14] = jnp.zeros((2, BZ, WIDE), bf16)
    for d in range(2):
        unsent = slice(COLS, WIDE) if d == 0 else slice(0, COLS)
        rb2[d, 0, :, unsent] = jnp.zeros((BY, COLS), bf16)
        rb3[d, 0, :, unsent] = jnp.zeros((BZ, COLS), bf16)
    edges[NZ] = jnp.zeros((2, SUBP, 8, 128), f32)
    compress(0)
    pl.semaphore_wait(barrier, 4 + NLEAF - 1)
    a_copy.start()
    exchange(0).start()

    a_copy.wait()
    for ref, low, count in ((ay, 0, BY), (az, BY, BZ)):
        for part in range(2):
            rows = slice(128 * part + low, 128 * part + low + count)
            mine, other = a_ref[rows], aoth[rows]
            ref[part * count : (part + 1) * count, 0:128] = mine
            ref[part * count : (part + 1) * count, 128:256] = other
            ref[(2 + part) * count : (3 + part) * count, 0:128] = mine
            ref[(2 + part) * count : (3 + part) * count, 128:256] = -other

    def partial_image(ref, low, count, tile, adds, put):
        par = tile % 2
        beams = slice(low, low + count)
        for at in range(0, COLS, 256):
            cols = slice(at, at + 256)
            imag = slice(COLS + at, COLS + at + 256)
            data = xb[tile, 0:2, :, cols].reshape(256, 256)
            r = jnp.dot(ref[...], data, preferred_element_type=f32)
            c, s = d0_ref[0, par, beams, cols], d0_ref[1, par, beams, cols]
            re = c * r[0:count] - s * r[3 * count :]
            im = c * r[count : 2 * count] + s * r[2 * count : 3 * count]
            for got in adds:
                re = re + got[:, cols].astype(f32)
                im = im + got[:, imag].astype(f32)
            put(cols, re)
            put(imag, im)

    def put_to(ref):
        def put(cols, value):
            ref[:, cols] = value.astype(ref.dtype)
        return put

    def y_to(d):
        return turn_at(z, y + 1 + 2 * d)

    def z_to(d):
        return turn_at(z + 1 + (NZ - 2) * d, y)

    def y_copy(d, k):
        return remote(sby.at[d, k], rby.at[d, k], y_s.at[d, k], y_r.at[d, k], {"turn": y_to(d)})

    def z_copy(d, k):
        return remote(sbz.at[d, k], rbz.at[d, k], z_s.at[d, k], z_r.at[d, k], {"turn": z_to(d)})

    def y_message(c, near, d):
        k = jnp.where(near == 1, 4 + c, c // 2)
        takes = (near == 1) & (c % 2 == d)
        src = jnp.where(takes, c // 2, 12)

        @pl.when(takes)
        def _():
            y_copy(d, c // 2).wait_recv()

        tile = turn_at(chunk(c), y + 2 + near * (2 * d - 1))
        partial_image(ay, 0, BY, tile, (rby.at[d, src],), put_to(sby.at[d, k]))
        y_copy(d, k).start()

    def z_far(d, j):
        tile = turn_at(chunk(0), y + order(j + 2 * d, NY))
        partial_image(az, BY, BZ, tile, (), put_to(sbz.at[d, j]))
        z_copy(d, j).start()

    def z_near(c, j):
        d = (c + 1) % 2
        step = (c - 1) // 2
        k = 2 + 4 * step + j
        takes = (step > 0) | (j // 2 == d)
        prev = jnp.where(step > 0, k - 4, j - 2 * d)
        src = jnp.where(takes, prev, 14)

        @pl.when(takes)
        def _():
            z_copy(d, prev).wait_recv()

        tile = turn_at(chunk(c), y + order(j, NY))
        partial_image(az, BY, BZ, tile, (rbz.at[d, src],), put_to(sbz.at[d, k]))
        z_copy(d, k).start()

    halves = (slice(0, COLS), slice(COLS, WIDE))

    def far2(d):
        part = halves[d]
        return remote(sb2.at[d, 0, :, part], rb2.at[d, 0, :, part], s2_s.at[d, 0], s2_r.at[d, 0], {"turn": z_to(d)})

    def near2(d, k):
        return remote(sb2.at[d, k], rb2.at[d, k], s2_s.at[d, k], s2_r.at[d, k], {"turn": z_to(d)})

    def far3(d):
        part = halves[d]
        return remote(sb3.at[d, 0, :, part], rb3.at[d, 0, :, part], s3_s.at[d, 0], s3_r.at[d, 0], {"turn": y_to(d)})

    def near3(d, k):
        return remote(sb3.at[d, k], rb3.at[d, k], s3_s.at[d, k], s3_r.at[d, k], {"turn": y_to(d)})

    def wait_y(i):
        for d in range(2):
            y_copy(d, 4 + i).wait_recv()
        return (rby.at[0, 4 + i], rby.at[1, 4 + i])

    def wait_z(i):
        for d in range(2):
            z_copy(d, 10 + i).wait_recv()
        return (rbz.at[0, 10 + i], rbz.at[1, 10 + i])

    def put_both(ref):
        def put(cols, value):
            d = 0 if cols.start < COLS else 1
            ref[d, 0, :, cols] = value.astype(bf16)
        return put

    def second_far():
        partial_image(ay, 0, BY, turn_at(z + 4, y), wait_y(0), put_both(sb2))
        for d in range(2):
            far2(d).start()

    def second_y(i):
        d = (i + 1) % 2
        q = (i - 1) // 2
        adds = wait_y(i)
        for side in range(2):
            @pl.when((q == 0) & (d == side))
            def _():
                far2(side).wait_recv()

        @pl.when(q > 0)
        def _():
            near2(d, q).wait_recv()

        partial_image(ay, 0, BY, turn_at(chunk(i), y), adds + (rb2.at[d, q],), put_to(sb2.at[d, q + 1]))
        near2(d, q + 1).start()

    def second_z(i):
        adds = wait_z(i)
        tile = turn_at(z, y + (2, 1, 3, 0)[i])
        if i == 0:
            partial_image(az, BY, BZ, tile, adds, put_both(sb3))
            for d in range(2):
                far3(d).start()
        elif i < 3:
            d = i - 1
            far3(d).wait_recv()
            partial_image(az, BY, BZ, tile, adds + (rb3.at[d, 0],), put_to(sb3.at[d, 1]))
            near3(d, 1).start()
        else:
            for d in range(2):
                near3(d, 1).wait_recv()
            adds = adds + (rb3.at[0, 1], rb3.at[1, 1])
            partial_image(az, BY, BZ, tile, adds, put_to(img.at[pl.ds(BY, BZ)]))

    def main_loop(i, carry):
        @pl.when(i < NZ)
        def _():
            compress(i)
            exchange(i).start()

        @pl.when(i <= NZ)
        def _():
            c = i - 1
            exchange(c).wait_recv()

            def pair(near, carry):
                y_message(c, near, (c + near) % 2)
                return carry

            lax.fori_loop(0, jnp.where(c < 2, 2, 1), pair, 0)

        @pl.when(i == 1)
        def _():
            def far(n, carry):
                z_far(n // 2, n % 2)
                return carry

            lax.fori_loop(0, 4, far, 0)

        @pl.when((i >= 4) & (i <= 9))
        def _():
            def near(j, carry):
                z_near(i - 3, j)
                return carry

            lax.fori_loop(0, 4, near, 0)

        @pl.when((i >= 4) & (i < 12))
        def _():
            def pair(n, carry):
                y_message(i - 4, 1, (i - 4 + n) % 2)
                return carry

            lax.fori_loop(0, jnp.where(i < 6, 1, 2), pair, 0)

        @pl.when(i == 6)
        def _():
            second_far()

        @pl.when((i > 6) & (i <= 12))
        def _():
            second_y(i - 6)

        @pl.when(i == 10)
        def _():
            second_z(0)

        @pl.when(i == 11)
        def _():
            second_z(1)

        @pl.when(i == 13)
        def _():
            second_z(2)

        @pl.when(i == 13)
        def _():
            beam = iota((BEAMS, 128), 0)
            odd = 2 * beam + 1 - BEAMS
            bins = iota((BEAMS, 128), 1) + 1 + COLS * core + 2 * COLS * turn
            for level in (1, 2):
                side = (leaf >> level) % 2
                i12[level - 1] = interp(taps_ref[level, side])
                rate = odd * ((2 * side - 1) * (level + 2))
                blocks = phase_blocks(rate * bins + beam * beam * (side + 1), rate * 128, COLS // 128)
                for b, (c, s) in enumerate(blocks):
                    at = slice(128 * b, 128 * b + 128)
                    d12[level - 1, 0, :, at] = c
                    d12[level - 1, 1, :, at] = s

        return carry

    lax.fori_loop(1, 14, main_loop, 0)
    second_z(3)
    adds = wait_y(7)
    for d in range(2):
        near2(d, 3).wait_recv()
    partial_image(ay, 0, BY, turn, adds + (rb2.at[0, 3], rb2.at[1, 3]), put_to(img.at[pl.ds(0, BY)]))

    for level in range(2):
        value = img[...]
        high = value.astype(bf16)
        low = (value - high.astype(f32)).astype(bf16)
        matrix = i12[level]
        moved = jnp.dot(matrix, high, preferred_element_type=f32) + jnp.dot(matrix, low, preferred_element_type=f32)
        c, s = d12[level, 0], d12[level, 1]
        re = c * moved[:, :COLS] - s * moved[:, COLS:]
        im = c * moved[:, COLS:] + s * moved[:, :COLS]
        target = img if level == 0 else vout
        target[:, :COLS] = re.astype(target.dtype)
        target[:, COLS:] = im.astype(target.dtype)

    def share(e):
        to = (leaf + e) % NLEAF
        rows = pl.ds(pl.multiple_of(16 * to, 16), 16)
        return remote(vout.at[rows], rl.at[leaf], l_s.at[e - 1], l_r.at[e - 1], {"leaf": to})

    def shared(e):
        src = (leaf + NLEAF - e) % NLEAF
        return remote(vout.at[pl.ds(0, 16)], rl.at[src], l_s.at[e - 1], l_r.at[e - 1], {"leaf": mate})

    for e in range(1, NLEAF):
        share(e).start()
    rl[leaf] = vout[pl.ds(pl.multiple_of(16 * leaf, 16), 16)]
    def sent_y(k, carry):
        for d in range(2):
            y_copy(d, k).wait_send()
        return carry

    def sent_z(k, carry):
        for d in range(2):
            z_copy(d, k).wait_send()
        return carry

    def sent_mate(i, carry):
        exchange(i).wait_send()
        return carry

    lax.fori_loop(0, NZ, sent_mate, 0)
    lax.fori_loop(0, 12, sent_y, 0)
    lax.fori_loop(0, 14, sent_z, 0)
    for d in range(2):
        far2(d).wait_send()
        far3(d).wait_send()
        near3(d, 1).wait_send()
        for k in range(1, 4):
            near2(d, k).wait_send()

    for e in range(1, NLEAF):
        shared(e).wait_recv()
    for side in range(2):
        total = rl[side].astype(f32)
        for xx in range(1, 4):
            total = total + rl[2 * xx + side].astype(f32)
        total = total.astype(bf16)
        for b in range(4):
            out_ref[4 * side + b, :, 0:128] = total[:, 128 * b : 128 * b + 128]
            out_ref[4 * side + b, :, 128:256] = total[:, COLS + 128 * b : COLS + 128 * b + 128]

    for e in range(1, NLEAF):
        share(e).wait_send()


def reduce_merge(x, chirp, taps, slots):
    vmem = pl.BlockSpec(memory_space=pltpu.VMEM)
    dma = pltpu.SemaphoreType.DMA
    return pl.pallas_call(
        main_kernel,
        out_shape=jax.ShapeDtypeStruct((8, 16, 256), bf16),
        in_specs=[pl.BlockSpec(memory_space=pl.ANY), vmem, vmem, pl.BlockSpec(memory_space=pltpu.SMEM)],
        out_specs=vmem,
        scratch_shapes=[
            pltpu.VMEM((2, 2, SUBP, GRAN, 256), bf16),
            pltpu.VMEM((2, SUBP, 8, 256), bf16),
            pltpu.VMEM((4, 2, 2, SUBP * 8 // 4, 128), f32),
            pltpu.VMEM((2, SUBP, 8, 128), f32),
            pltpu.VMEM((NZ + 1, 2, SUBP, 8, 128), f32),
            pltpu.VMEM((TILES, 3, 128, COLS), bf16),
            pltpu.VMEM((256, 128), bf16),
            pltpu.VMEM((4 * BY, 256), bf16),
            pltpu.VMEM((4 * BZ, 256), bf16),
            pltpu.VMEM((2, 13, BY, WIDE), bf16),
            pltpu.VMEM((2, 12, BY, WIDE), bf16),
            pltpu.VMEM((2, 15, BZ, WIDE), bf16),
            pltpu.VMEM((2, 14, BZ, WIDE), bf16),
            pltpu.VMEM((2, 4, BY, WIDE), bf16),
            pltpu.VMEM((2, 4, BY, WIDE), bf16),
            pltpu.VMEM((2, 2, BZ, WIDE), bf16),
            pltpu.VMEM((2, 2, BZ, WIDE), bf16),
            pltpu.VMEM((BEAMS, WIDE), f32),
            pltpu.VMEM((BEAMS, WIDE), bf16),
            pltpu.VMEM((NLEAF, 16, WIDE), bf16),
            pltpu.VMEM((2, BEAMS, BEAMS), bf16),
            pltpu.VMEM((2, 2, BEAMS, COLS), f32),
            pltpu.VMEM((256, 512), bf16),
            pltpu.VMEM((256, 128), bf16),
            pltpu.VMEM((2, 2, BEAMS, COLS), f32),
            dma((2, 2)), dma((2,)), dma((NZ,)), dma((NZ,)), dma, dma,
            dma((2, 12)), dma((2, 12)), dma((2, 14)), dma((2, 14)),
            dma((2, 4)), dma((2, 4)), dma((2, 2)), dma((2, 2)),
            dma((NLEAF - 1,)), dma((NLEAF - 1,)),
        ],
        compiler_params=pltpu.CompilerParams(
            collective_id=0, has_side_effects=True, vmem_limit_bytes=60 * 1024 * 1024
        ),
        name="reduce_merge",
    )(x, chirp, taps, slots)


def per_device(echoes, chirp, taps, slots):
    taps = jnp.transpose(taps, (0, 1, 3, 2))
    image = reduce_merge(echoes, chirp, taps, slots)
    return jnp.transpose(image, (1, 0, 2))


def solution(mesh):
    placed = (P(("leaf", "turn"), None, None), P(), P(), P("leaf", None))
    return jax.shard_map(
        per_device, mesh=mesh, in_specs=placed, out_specs=P("leaf", "turn", None), check_vma=False
    )
```
